32 devices in a mesh: shard: 4 (over z), ctx: 4 (over x, core), tp: 2 (over y).
Axes of the slice: x: 2, y: 2, z: 4, core: 2. Of those that a mesh axis runs over, the one named last changes fastest.
Arguments:
- inputs: bfloat16 [4, 2048, 2048], P('shard', 'ctx'), may hold values from -6 to 6
- cotangent: bfloat16 [4, 2048, 2048], P('shard', 'ctx'), may hold values from -6 to 6
- query_weight: bfloat16 [2048, 2048], P('shard', 'tp'), may hold values from -0.1875 to 0.1875
- key_weight: bfloat16 [2048, 2048], P('shard', 'tp'), may hold values from -0.1875 to 0.1875
- value_weight: bfloat16 [2048, 2048], P('shard', 'tp'), may hold values from -0.125 to 0.125
- output_weight: bfloat16 [2048, 2048], P('shard', 'tp'), may hold values from -0.75 to 0.75
- up_weight: bfloat16 [2048, 8192], P('shard', 'tp'), may hold values from -0.125 to 0.125
- down_weight: bfloat16 [2048, 8192], P('shard', 'tp'), may hold values from -0.0625 to 0.0625
- query_value_bias: bfloat16 [2, 16, 128], P(None, 'tp', 'shard'), may hold values from -3 to 3
- up_bias: bfloat16 [64, 128], P('tp', 'shard'), may hold values from -3 to 3
- norm_gains: bfloat16 [2, 16, 128], P(None, 'tp', 'shard'), may hold values from 0.25 to 1.75
- other_biases: bfloat16 [4, 16, 128], P(None, 'tp', 'shard'), may hold values from -2 to 2
Outputs:
- outputs: bfloat16 [4, 2048, 2048], P('shard', 'ctx')
- input_grad: bfloat16 [4, 2048, 2048], P('shard', 'ctx')
- grad_query: float32 [2048, 2048], P('shard', 'tp')
- grad_key: float32 [2048, 2048], P('shard', 'tp')
- grad_value: float32 [2048, 2048], P('shard', 'tp')
- grad_output: float32 [2048, 2048], P('shard', 'tp')
- grad_up: float32 [2048, 8192], P('shard', 'tp')
- grad_down: float32 [2048, 8192], P('shard', 'tp')
- grad_qv_bias: float32 [2, 16, 128], P(None, 'tp', 'shard')
- grad_up_bias: float32 [64, 128], P('tp', 'shard')
- grad_gains: float32 [2, 16, 128], P(None, 'tp', 'shard')
- grad_biases: float32 [4, 16, 128], P(None, 'tp', 'shard')
- root_squares: float32 [3], replicated
The draws below stay inside these ranges and needn't reach their ends.
All inputs are finite; a program needn't handle non-finite values.
Results may differ from the reference program's by a relative error of at most 0.024.
Values may be sent and summed in bfloat16 or wider, within the bound.
No kernel may reach another device: no remote copies, remote signals or barrier semaphores. Data moves between devices by JAX's collectives and lax.ppermute only.
A program may use at most 320 MiB of HBM per device.

```python
import jax
import jax.numpy as jnp
from jax import lax

D = 2048
H = 16
FF = 8192
DH = 128
SEQ_LEN = 2048
SEQS = 4


def level_of(key, shape, cuts, least, high):
    level = 1.0
    for axis_at, blocks in cuts:
        steps = jax.random.uniform(jax.random.fold_in(jax.random.fold_in(key, 6), axis_at), (blocks,), jnp.float32, least / len(cuts), high / len(cuts))
        level = level * jnp.repeat(jnp.exp(steps), shape[axis_at] // blocks).reshape((-1,) + (1,) * (len(shape) - 1 - axis_at))
    return level


def gaussian(stream_key, extent, spread, limit, cuts=(), dtype=jnp.bfloat16):
    array = jax.random.normal(stream_key, extent, jnp.float32) * spread
    if len(cuts) > 0:
        array = level_of(stream_key, extent, cuts, -0.22, 0.18) * array
    return jnp.clip(array, min=-limit, max=limit).astype(dtype)


def setup_inputs(seed: int = 0) -> dict:
    key_list = jax.random.split(jax.random.key(seed), 13)
    return {
        "inputs": gaussian(key_list[0], (SEQS, SEQ_LEN, D), 1.0, 6.0, ((0, 4), (1, 4))),
        "cotangent": gaussian(key_list[1], (SEQS, SEQ_LEN, D), 1.0, 6.0, ((0, 4), (1, 4))),
        "query_weight": gaussian(key_list[2], (D, D), (D // 2) ** -0.5, 0.1875, ((0, 4), (1, 2))),
        "key_weight": gaussian(key_list[3], (D, D), (D // 2) ** -0.5, 0.1875, ((0, 4), (1, 2))),
        "value_weight": gaussian(key_list[4], (D, D), D ** -0.5, 0.125, ((0, 4), (1, 2))),
        "output_weight": gaussian(key_list[5], (D, D), (D // 32) ** -0.5, 0.75, ((0, 4), (1, 2))),
        "up_weight": gaussian(key_list[6], (D, FF), D ** -0.5, 0.125, ((0, 4), (1, 2))),
        "down_weight": gaussian(key_list[7], (D, FF), FF ** -0.5, 0.0625, ((0, 4), (1, 2))),
        "query_value_bias": gaussian(key_list[8], (2, H, DH), 0.5, 3.0, ((1, 2), (2, 4))),
        "up_bias": gaussian(key_list[9], (FF // DH, DH), 0.5, 3.0, ((0, 2), (1, 4))),
        "norm_gains": jnp.clip(1.0 + 0.15 * jax.random.normal(key_list[10], (2, H, DH), jnp.float32), 0.25, 1.75).astype(jnp.bfloat16),
        "other_biases": gaussian(key_list[11], (4, H, DH), 0.3, 2.0, ((1, 2), (2, 4))),
    }


@jax.custom_vjp
def low(v):
    return lax.optimization_barrier(v.astype(jnp.bfloat16)).astype(jnp.float32)

@jax.custom_vjp
def low_back(v):
    return v

def low_keep(v):
    return (low(v), None)

def low_pass(kept, grad):
    return (grad,)

def back_keep(v):
    return (v, None)

def back_low(kept, grad):
    return (low(grad),)
low.defvjp(low_keep, low_pass)
low_back.defvjp(back_keep, back_low)
epsilon = 1e-12
highest = lax.Precision.HIGHEST

def matmul(left, right):
    return jnp.dot(left, right, precision=highest)

def matmul_nt(left, right):
    return lax.dot_general(left, right, (((1,), (1,)), ((), ())), precision=highest)

def normalize(stream):
    center = stream - lax.optimization_barrier(jnp.mean(stream, axis=-1, keepdims=True))
    return center * lax.rsqrt(lax.optimization_barrier(jnp.mean(center * center, axis=-1, keepdims=True)) + epsilon)

def head_attention(triple):
    queries, keys, values = triple
    scores = low_back(matmul_nt(queries, keys) * DH ** (-0.5))
    probs = jax.nn.softmax(scores, axis=-1)
    return matmul(low(probs), values)

def sequence_layer(stream, params):
    query_w, key_w, value_w, output_w, up_w, down_w, qv_bias, up_b, gains, biases = params
    length = stream.shape[0]
    qv_flat = qv_bias.reshape(2, D)
    gain_flat = gains.reshape(2, D)
    bias_flat = biases.reshape(4, D)
    queries = low_back(low(matmul(stream, query_w) + qv_flat[0]))
    keys = low_back(low(matmul(stream, key_w)))
    values = low_back(low(matmul(stream, value_w) + qv_flat[1]))

    def split_heads(matrix):
        return matrix.reshape(length, H, DH).transpose(1, 0, 2)
    head_out = lax.map(jax.checkpoint(head_attention), (split_heads(queries), split_heads(keys), split_heads(values)))
    attended = low_back(low(head_out.transpose(1, 0, 2).reshape(length, D)))
    attn_branch = low_back(matmul_nt(attended, output_w) + bias_flat[0])
    hidden_one = normalize(stream + attn_branch) * gain_flat[0] + bias_flat[1]
    pre_act = low_back(matmul(low(hidden_one), up_w) + up_b.reshape(FF))
    activated = low(jax.nn.gelu(pre_act, approximate=True))
    mlp_branch = low_back(matmul_nt(activated, down_w) + bias_flat[2])
    second = hidden_one + mlp_branch
    result = normalize(second) * gain_flat[1] + bias_flat[3]
    sums = jnp.stack([jnp.sum(second * second), jnp.sum(attn_branch * attn_branch), jnp.sum(mlp_branch * mlp_branch)])
    return (result, sums)

def reference(inputs, cotangent, query_weight, key_weight, value_weight, output_weight, up_weight, down_weight, query_value_bias, up_bias, norm_gains, other_biases):
    floats = [item.astype(jnp.float32) for item in (inputs, query_weight, key_weight, value_weight, output_weight, up_weight, down_weight, query_value_bias, up_bias, norm_gains, other_biases)]

    def forward(stream_all, *params):

        def single(stream):
            return sequence_layer(stream, params)
        results, sums = lax.map(single, stream_all)
        return (results, lax.optimization_barrier(jnp.sum(sums, axis=0)))
    result, pullback, sums = jax.vjp(forward, *floats, has_aux=True)
    grads = pullback(cotangent.astype(jnp.float32))
    count = inputs.shape[0] * inputs.shape[1] * D
    root_squares = jnp.sqrt(sums / count)
    return (result.astype(jnp.bfloat16), grads[0].astype(jnp.bfloat16), grads[1], grads[2], grads[3], grads[4], grads[5], grads[6], grads[7], grads[8], grads[9], grads[10], root_squares)
```

```python
import jax
import jax.numpy as jnp
from jax import lax
from jax.sharding import PartitionSpec as P

D = 2048
H = 16
DH = 128
SCALE = DH ** (-0.5)
BF = jnp.bfloat16
F32 = jnp.float32


epsilon = 1e-12


def product(left, right):
    return jnp.dot(left, right, preferred_element_type=F32)


def times_transposed(left, right):
    return lax.dot_general(left, right, (((1,), (1,)), ((), ())), preferred_element_type=F32)


def transposed_times(left, right):
    return lax.dot_general(left, right, (((0,), (0,)), ((), ())), preferred_element_type=F32)


def normalize(stream):
    center = stream - jnp.mean(stream, axis=-1, keepdims=True)
    factor = lax.rsqrt(jnp.mean(center * center, axis=-1, keepdims=True) + epsilon)
    return (center * factor, factor)


def norm_backward(grad_norm, normed, factor):
    return factor * (
        grad_norm
        - jnp.mean(grad_norm, axis=-1, keepdims=True)
        - normed * jnp.mean(grad_norm * normed, axis=-1, keepdims=True)
    )


def gelu_tanh(values):
    return jax.nn.gelu(values, approximate=True)


def head_forward(triple):
    q_head, k_head, v_head = triple
    scores = times_transposed(q_head, k_head) * SCALE
    peak = jnp.max(scores, axis=-1, keepdims=True)
    expo = jnp.exp(scores - peak)
    total = jnp.sum(expo, axis=-1, keepdims=True)
    probs = expo / total
    result = product(probs.astype(BF), v_head)
    return (result, (peak + jnp.log(total))[:, 0])


def head_backward(group):
    q_head, k_head, v_head, d_head, logsum = group
    scores = times_transposed(q_head, k_head) * SCALE
    probs = jnp.exp(scores - logsum[:, None])
    d_probs = times_transposed(d_head, v_head)
    inner = jnp.sum(probs * d_probs, axis=-1, keepdims=True)
    d_scores = (probs * (d_probs - inner)).astype(BF)
    d_query = product(d_scores, k_head) * SCALE
    d_key = transposed_times(d_scores, q_head) * SCALE
    d_value = transposed_times(probs.astype(BF), d_head)
    return (d_query.astype(BF), d_key.astype(BF), d_value.astype(BF))


def across(array, step, axis="ctx"):
    size = lax.axis_size(axis)
    return lax.ppermute(array, axis, [(at, at ^ step) for at in range(size)])


def gather_columns(piece):
    own = lax.all_gather(piece, "shard", axis=0, tiled=True)
    far = across(own, 2)
    return [own, across(own, 1), far, across(far, 1)]


def reduce_columns(parts):
    near_own = across(parts[1], 1)
    near_far = across(parts[3], 1)
    far = (parts[2].astype(F32) + near_far.astype(F32)).astype(BF)
    own = parts[0].astype(F32) + near_own.astype(F32)
    total = (own + across(far, 2).astype(F32)).astype(BF)
    mine = lax.psum_scatter(total, "shard", scatter_dimension=0, tiled=True)
    other = across(mine, 2)
    return [mine, across(mine, 1), other, across(other, 1)]


def ordered(pieces, bits):
    low, high = bits
    swapped = [jnp.where(high, pieces[q ^ 2], pieces[q]) for q in range(4)]
    return [jnp.where(low, swapped[q ^ 1], swapped[q]) for q in range(4)]


def tp_sum(part):
    low = part.astype(BF)
    return low.astype(F32) + across(low, 1, "tp").astype(F32)


def butterfly(flat):
    for axis in ("ctx", "shard"):
        step = 1
        while step < lax.axis_size(axis):
            flat = flat + across(flat, step, axis)
            step *= 2
    return flat


def shards(
    inputs,
    cotangent,
    query_weight,
    key_weight,
    value_weight,
    output_weight,
    up_weight,
    down_weight,
    query_value_bias,
    up_bias,
    norm_gains,
    other_biases,
):
    local_rows = inputs.shape[1]
    member = lax.axis_index("ctx")
    relative = jnp.arange(4) ^ member
    bits = ((member & 1) == 1, (member & 2) == 2)
    n_shard = lax.axis_size("shard")
    n_tp = lax.axis_size("tp")

    def own_columns(weight):
        width = weight.shape[1] // 4
        return lax.dynamic_slice_in_dim(weight, member * width, width, 1)

    tokens = inputs.reshape(local_rows, D)
    tokens_far = across(tokens, 2)
    grad_out = cotangent.reshape(local_rows, D).astype(F32)

    small = (query_value_bias, norm_gains, other_biases, up_bias)
    packed = jnp.concatenate([item.reshape(-1) for item in small])
    packed_all = lax.all_gather(packed, ("shard", "tp"), axis=0, tiled=False)
    packed_all = packed_all.reshape(n_shard, n_tp, packed.shape[0])
    at = 0
    small_all = []
    for item in small:
        part = packed_all[:, :, at : at + item.size].reshape((n_shard, n_tp) + item.shape)
        at += item.size
        small_all.append(part)
    tp_index = lax.axis_index("tp")
    qv_all = lax.dynamic_index_in_dim(small_all[0], tp_index, 1, False)
    qv_half = qv_all.transpose(1, 2, 0, 3).reshape(2, 4, -1).astype(F32)
    qv_vector = jnp.take(qv_half, relative, axis=1)
    gains = small_all[1].transpose(2, 1, 3, 0, 4).reshape(2, D).astype(F32)
    biases = small_all[2].transpose(2, 1, 3, 0, 4).reshape(4, D).astype(F32)
    up_all = lax.dynamic_index_in_dim(small_all[3], tp_index, 1, False)
    up_vector = jnp.take(up_all.transpose(1, 0, 2).reshape(4, -1).astype(F32), relative, axis=0)

    kv_width = key_weight.shape[1] // 4
    key_value_w = gather_columns(
        jnp.concatenate([own_columns(key_weight), own_columns(value_weight)], axis=1)
    )
    query_w = gather_columns(own_columns(query_weight))
    output_w = gather_columns(own_columns(output_weight))
    up_w = gather_columns(own_columns(up_weight))
    down_w = gather_columns(own_columns(down_weight))

    tokens_two = jnp.concatenate([tokens, tokens_far], axis=0)
    zero_row = jnp.zeros((kv_width,), F32)
    kv_here = jnp.stack(
        [
            (
                product(tokens_two, key_value_w[q])
                + jnp.concatenate([zero_row, qv_vector[1, q]])
            ).astype(BF)
            for q in range(4)
        ]
    )
    kv_near = across(kv_here, 1)
    queries = [(product(tokens, query_w[q]) + qv_vector[0, q]).astype(BF) for q in range(4)]
    heads_each = kv_width // DH
    query_heads, key_heads, value_heads = [], [], []
    for q in range(4):
        both = jnp.concatenate([kv_here[q], kv_near[q ^ 1]], axis=0)
        for j in range(heads_each):
            query_heads.append(queries[q][:, j * DH : (j + 1) * DH])
            key_heads.append(both[:, j * DH : (j + 1) * DH])
            value_heads.append(both[:, kv_width + j * DH : kv_width + (j + 1) * DH])
    query_heads = jnp.stack(query_heads)
    key_heads = jnp.stack(key_heads)
    value_heads = jnp.stack(value_heads)
    heads_here = query_heads.shape[0]
    head_out, logsums = lax.map(head_forward, (query_heads, key_heads, value_heads))
    attended = head_out.transpose(1, 0, 2).reshape(local_rows, heads_here * DH).astype(BF)
    output_full = jnp.concatenate(output_w, axis=1)
    attn_branch = tp_sum(times_transposed(attended, output_full)) + biases[0]
    normed_one, factor_one = normalize(tokens.astype(F32) + attn_branch)
    hidden_one = normed_one * gains[0] + biases[1]
    hidden_low = hidden_one.astype(BF)

    pre_act = [product(hidden_low, up_w[q]) + up_vector[q] for q in range(4)]
    activated = [gelu_tanh(pre_act[q]).astype(BF) for q in range(4)]
    mlp_part = sum(times_transposed(activated[q], down_w[q]) for q in range(4))
    mlp_branch = tp_sum(mlp_part) + biases[2]
    second = hidden_one + mlp_branch
    normed_two, factor_two = normalize(second)
    result = normed_two * gains[1] + biases[3]
    grad_second = norm_backward(grad_out * gains[1], normed_two, factor_two)
    grad_mlp = grad_second.astype(BF)
    down_grads = reduce_columns(
        [transposed_times(grad_mlp, activated[q]).astype(BF) for q in range(4)]
    )
    grad_pre = []
    for q in range(4):
        unused, gelu_pull = jax.vjp(gelu_tanh, pre_act[q])
        grad_pre.append(gelu_pull(product(grad_mlp, down_w[q]))[0].astype(BF))
    hidden_part = sum(times_transposed(grad_pre[q], up_w[q]) for q in range(4))
    grad_hidden = grad_second + tp_sum(hidden_part)
    up_grads = reduce_columns(
        [transposed_times(hidden_low, grad_pre[q]).astype(BF) for q in range(4)]
    )
    grad_first = norm_backward(grad_hidden * gains[0], normed_one, factor_one)
    grad_branch = grad_first.astype(BF)
    grad_attended = product(grad_branch, output_full).astype(BF)
    quarter = heads_each * DH
    output_grads = reduce_columns(
        [
            transposed_times(grad_branch, attended[:, q * quarter : (q + 1) * quarter]).astype(BF)
            for q in range(4)
        ]
    )
    grad_heads = grad_attended.reshape(local_rows, heads_here, DH).transpose(1, 0, 2)
    dq_heads, dk_heads, dv_heads = lax.map(
        head_backward, (query_heads, key_heads, value_heads, grad_heads, logsums)
    )
    dkv = jnp.stack(
        [
            jnp.concatenate(
                [dk_heads[q * heads_each + j] for j in range(heads_each)]
                + [dv_heads[q * heads_each + j] for j in range(heads_each)],
                axis=1,
            )
            for q in range(4)
        ]
    )
    near = across(dkv[:, 2 * local_rows :], 1)
    dkv_two = jnp.stack(
        [
            (dkv[q, : 2 * local_rows].astype(F32) + near[q ^ 1].astype(F32)).astype(BF)
            for q in range(4)
        ]
    )
    far = across(dkv_two[:, local_rows:], 2)
    grad_kv = [
        (dkv_two[q, :local_rows].astype(F32) + far[q ^ 2].astype(F32)).astype(BF) for q in range(4)
    ]
    grad_q = [
        jnp.concatenate([dq_heads[q * heads_each + j] for j in range(heads_each)], axis=1)
        for q in range(4)
    ]
    query_grads = reduce_columns([transposed_times(tokens, grad_q[q]).astype(BF) for q in range(4)])
    kv_grads = reduce_columns([transposed_times(tokens, grad_kv[q]).astype(BF) for q in range(4)])
    input_part = sum(
        times_transposed(grad_q[q], query_w[q]) + times_transposed(grad_kv[q], key_value_w[q])
        for q in range(4)
    )
    input_grad = grad_first + tp_sum(input_part)

    def canonical(rows):
        return jnp.take(jnp.stack(rows), relative, axis=0).reshape(-1)

    def column_sums(array):
        return jnp.sum(array.astype(F32), axis=0)

    pieces = [
        canonical([column_sums(grad_q[q]) for q in range(4)]),
        canonical([column_sums(grad_kv[q][:, kv_width:]) for q in range(4)]),
        canonical([column_sums(grad_pre[q]) for q in range(4)]),
        jnp.sum(grad_hidden * normed_one, axis=0),
        jnp.sum(grad_out * normed_two, axis=0),
        column_sums(grad_branch),
        jnp.sum(grad_hidden, axis=0),
        column_sums(grad_mlp),
        jnp.sum(grad_out, axis=0),
        jnp.stack(
            [
                jnp.sum(second * second),
                jnp.sum(attn_branch * attn_branch),
                jnp.sum(mlp_branch * mlp_branch),
            ]
        ),
    ]
    sizes = [item.shape[0] for item in pieces]
    flat = jnp.concatenate(pieces + [jnp.zeros((-sum(sizes) % 1024,), F32)]).reshape(-1, 128)
    flat = butterfly(flat).reshape(-1)
    totals = []
    at = 0
    for size in sizes:
        totals.append(flat[at : at + size])
        at += size
    shard_index = lax.axis_index("shard")
    piece = DH // n_shard
    heads_part = H // n_tp

    def last_piece(array, axis):
        return lax.dynamic_slice_in_dim(array, shard_index * piece, piece, axis)

    grad_qv_bias = last_piece(jnp.stack(totals[0:2]).reshape(2, heads_here, DH), 2)
    grad_up_bias = last_piece(totals[2].reshape(-1, DH), 1)

    def feature_rows(rows):
        stacked = jnp.stack(rows).reshape(len(rows), H, DH)
        return last_piece(
            lax.dynamic_slice_in_dim(stacked, tp_index * heads_part, heads_part, 1), 2
        )

    grad_gains = feature_rows(totals[3:5])
    grad_biases = feature_rows(totals[5:9])
    count_all = local_rows * n_shard * lax.axis_size("ctx") * D
    root_squares = jnp.sqrt(totals[9] / count_all)

    def whole(parts):
        return jnp.concatenate(ordered(parts, bits), axis=1).astype(F32)

    return (
        result.astype(BF).reshape(1, local_rows, D),
        input_grad.astype(BF).reshape(1, local_rows, D),
        whole(query_grads),
        whole([item[:, :kv_width] for item in kv_grads]),
        whole([item[:, kv_width:] for item in kv_grads]),
        whole(output_grads),
        whole(up_grads),
        whole(down_grads),
        grad_qv_bias,
        grad_up_bias,
        grad_gains,
        grad_biases,
        root_squares,
    )


def solution(mesh):
    if mesh.shape["ctx"] != 4 or mesh.shape["tp"] != 2:
        raise ValueError("unexpected mesh")
    placed = (
        P("shard", "ctx", None),
        P("shard", "ctx", None),
        P("shard", "tp"),
        P("shard", "tp"),
        P("shard", "tp"),
        P("shard", "tp"),
        P("shard", "tp"),
        P("shard", "tp"),
        P(None, "tp", "shard"),
        P("tp", "shard"),
        P(None, "tp", "shard"),
        P(None, "tp", "shard"),
    )
    return jax.shard_map(
        shards,
        mesh=mesh,
        in_specs=placed,
        out_specs=(
            P("shard", "ctx", None),
            P("shard", "ctx", None),
            P("shard", "tp"),
            P("shard", "tp"),
            P("shard", "tp"),
            P("shard", "tp"),
            P("shard", "tp"),
            P("shard", "tp"),
            P(None, "tp", "shard"),
            P("tp", "shard"),
            P(None, "tp", "shard"),
            P(None, "tp", "shard"),
            P(),
        ),
        check_vma=False,
    )
```

```python
import jax
import jax.numpy as jnp
from jax import lax
from jax.experimental import pallas as pl
from jax.experimental.pallas import tpu as pltpu
from jax.sharding import PartitionSpec as P

D = 2048
H = 16
DH = 128
SCALE = DH ** (-0.5)
BF = jnp.bfloat16
F32 = jnp.float32


epsilon = 1e-12


def product(left, right):
    return jnp.dot(left, right, preferred_element_type=F32)


def times_transposed(left, right):
    return lax.dot_general(left, right, (((1,), (1,)), ((), ())), preferred_element_type=F32)


def transposed_times(left, right):
    return lax.dot_general(left, right, (((0,), (0,)), ((), ())), preferred_element_type=F32)


def normalize(stream):
    center = stream - jnp.mean(stream, axis=-1, keepdims=True)
    factor = lax.rsqrt(jnp.mean(center * center, axis=-1, keepdims=True) + epsilon)
    return (center * factor, factor)


def norm_backward(grad_norm, normed, factor):
    return factor * (
        grad_norm
        - jnp.mean(grad_norm, axis=-1, keepdims=True)
        - normed * jnp.mean(grad_norm * normed, axis=-1, keepdims=True)
    )


def gelu_tanh(values):
    return jax.nn.gelu(values, approximate=True)


def contract(left, right, left_axis, right_axis):
    return lax.dot_general(
        left, right, (((left_axis,), (right_axis,)), ((), ())), preferred_element_type=F32
    )


def forward_kernel(q_ref, kh_ref, kn_ref, vh_ref, vn_ref, out_ref, log_ref):
    q = q_ref[...]
    near = contract(kh_ref[...], q, 1, 1) * SCALE
    far = contract(kn_ref[...], q, 1, 1) * SCALE
    peak = jnp.maximum(jnp.max(near, axis=0, keepdims=True), jnp.max(far, axis=0, keepdims=True))
    near = jnp.exp(near - peak)
    far = jnp.exp(far - peak)
    total = jnp.sum(near, axis=0, keepdims=True) + jnp.sum(far, axis=0, keepdims=True)
    out = contract(vh_ref[...], near.astype(BF), 0, 0) + contract(vn_ref[...], far.astype(BF), 0, 0)
    out_ref[...] = (out / total).T.astype(BF)
    log_ref[0] = peak + jnp.log(total)

def backward_kernel(q_ref, kh_ref, kn_ref, vh_ref, vn_ref, grad_ref, log_ref, dq_ref, dkh_ref, dkn_ref, dvh_ref, dvn_ref, *sums):
    step = pl.program_id(1)
    q = q_ref[...]
    grad = grad_ref[...]
    logsum = log_ref[0]
    probs, d_probs = [], []
    for k_ref, v_ref in ((kh_ref, vh_ref), (kn_ref, vn_ref)):
        probs.append(jnp.exp(contract(k_ref[...], q, 1, 1) * SCALE - logsum))
        d_probs.append(contract(v_ref[...], grad, 1, 1))
    inner = sum(jnp.sum(p * d, axis=0, keepdims=True) for p, d in zip(probs, d_probs))
    dq = 0.0
    for at, k_ref in enumerate((kh_ref, kn_ref)):
        d_scores = (probs[at] * (d_probs[at] - inner)).astype(BF)
        dq = dq + contract(k_ref[...], d_scores, 0, 0)
        dk = contract(d_scores, q, 1, 0)
        dv = contract(probs[at].astype(BF), grad, 1, 0)
        @pl.when(step == 0)
        def _():
            sums[at][...] = dk
            sums[2 + at][...] = dv
        @pl.when(step > 0)
        def _():
            sums[at][...] += dk
            sums[2 + at][...] += dv
    dq_ref[...] = (dq * SCALE).T.astype(BF)
    @pl.when(step == pl.num_programs(1) - 1)
    def _():
        dkh_ref[...] = (sums[0][...] * SCALE).astype(BF)
        dkn_ref[...] = (sums[1][...] * SCALE).astype(BF)
        dvh_ref[...] = sums[2][...].astype(BF)
        dvn_ref[...] = sums[3][...].astype(BF)

def kv_specs(rows, heads):
    k = pl.BlockSpec((rows, DH), lambda h, b: (0, h))
    v = pl.BlockSpec((rows, DH), lambda h, b: (0, heads + h))
    return k, k, v, v

def attention(q, kvh, kvn, block=None):
    rows, width = q.shape
    block = block or rows
    heads = width // DH
    row = pl.BlockSpec((block, DH), lambda h, b: (b, h))
    log = pl.BlockSpec((1, 1, block), lambda h, b: (h, 0, b))
    return pl.pallas_call(forward_kernel, grid=(heads, rows // block),
        in_specs=[row, *kv_specs(kvh.shape[0], heads)], out_specs=[row, log],
        out_shape=[jax.ShapeDtypeStruct((rows, width), BF), jax.ShapeDtypeStruct((heads, 1, rows), F32)],
        name="attention_forward")(q, kvh, kvn, kvh, kvn)

def attention_back(q, kvh, kvn, grad, logsum, block=None):
    rows, width = q.shape
    block = block or rows
    heads = width // DH
    keys = kvh.shape[0]
    row = pl.BlockSpec((block, DH), lambda h, b: (b, h))
    log = pl.BlockSpec((1, 1, block), lambda h, b: (h, 0, b))
    k = pl.BlockSpec((keys, DH), lambda h, b: (0, h))
    return pl.pallas_call(backward_kernel, grid=(heads, rows // block),
        in_specs=[row, *kv_specs(keys, heads), row, log],
        out_specs=[row, k, k, k, k],
        out_shape=[jax.ShapeDtypeStruct((rows, width), BF)] + [jax.ShapeDtypeStruct((keys, width), BF)] * 4,
        scratch_shapes=[pltpu.VMEM((keys, DH), F32)] * 4,
        name="attention_backward")(q, kvh, kvn, kvh, kvn, grad, logsum)


def sum_kernel(*refs):
    count = (len(refs) - 1) // 2
    total = 0.0
    for at in range(count):
        total = total + contract(refs[at][...], refs[count + at][...], 1, 1)
    refs[-1][...] = total.astype(refs[-1].dtype)


def sum_products(lefts, rights, block=256):
    rows = lefts[0].shape[0]
    width = rights[0].shape[0]
    return pl.pallas_call(
        sum_kernel,
        grid=(width // block,),
        in_specs=[pl.BlockSpec(left.shape, lambda n: (0, 0)) for left in lefts]
        + [pl.BlockSpec((block, right.shape[1]), lambda n: (n, 0)) for right in rights],
        out_specs=pl.BlockSpec((rows, block), lambda n: (0, n)),
        out_shape=jax.ShapeDtypeStruct((rows, width), BF),
        name="sum_products",
    )(*lefts, *rights)


def after(value, *others):
    return lax.optimization_barrier((value,) + others)[0]


def across(array, step, axis="ctx"):
    size = lax.axis_size(axis)
    return lax.ppermute(array, axis, [(at, at ^ step) for at in range(size)])


def collect(piece):
    return lax.all_gather(piece, "shard", axis=0, tiled=True)


def spread(own):
    far = across(own, 2)
    return [own, across(own, 1), far, across(far, 1)]


def reduce_columns(parts):
    near_own = across(parts[1], 1)
    near_far = across(parts[3], 1)
    far = (parts[2].astype(F32) + near_far.astype(F32)).astype(BF)
    own = parts[0].astype(F32) + near_own.astype(F32)
    total = (own + across(far, 2).astype(F32)).astype(BF)
    mine = lax.psum_scatter(total, "shard", scatter_dimension=0, tiled=True)
    other = across(mine, 2)
    return [mine, across(mine, 1), other, across(other, 1)]


def ordered(pieces, bits):
    low, high = bits
    swapped = [jnp.where(high, pieces[q ^ 2], pieces[q]) for q in range(4)]
    return [jnp.where(low, swapped[q ^ 1], swapped[q]) for q in range(4)]


def tp_sum(low):
    return low.astype(F32) + across(low, 1, "tp").astype(F32)


def butterfly(flat, axes):
    for axis in axes:
        step = 1
        while step < lax.axis_size(axis):
            flat = flat + across(flat, step, axis)
            step *= 2
    return flat


def shards(
    inputs,
    cotangent,
    query_weight,
    key_weight,
    value_weight,
    output_weight,
    up_weight,
    down_weight,
    query_value_bias,
    up_bias,
    norm_gains,
    other_biases,
):
    local_rows = inputs.shape[1]
    member = lax.axis_index("ctx")
    relative = jnp.arange(4) ^ member
    bits = ((member & 1) == 1, (member & 2) == 2)
    n_shard = lax.axis_size("shard")
    n_tp = lax.axis_size("tp")

    def own_columns(weight):
        width = weight.shape[1] // 4
        return lax.dynamic_slice_in_dim(weight, member * width, width, 1)

    tokens = inputs.reshape(local_rows, D)
    tokens_far = across(tokens, 2)
    grad_out = cotangent.reshape(local_rows, D).astype(F32)

    small = (query_value_bias, norm_gains, other_biases, up_bias)
    packed = jnp.concatenate([item.reshape(1, -1) for item in small], axis=1)
    tp_index = lax.axis_index("tp")
    slot = lax.axis_index("shard") * n_tp + tp_index
    packed_all = lax.dynamic_update_slice_in_dim(
        jnp.zeros((n_shard * n_tp, packed.shape[1]), BF), packed, slot, 0
    )
    packed_all = butterfly(packed_all, ("tp", "shard"))
    packed_all = packed_all.reshape(n_shard, n_tp, packed.shape[1])
    at = 0
    small_all = []
    for item in small:
        part = packed_all[:, :, at : at + item.size].reshape((n_shard, n_tp) + item.shape)
        at += item.size
        small_all.append(part)
    qv_all = lax.dynamic_index_in_dim(small_all[0], tp_index, 1, False)
    qv_half = qv_all.transpose(1, 2, 0, 3).reshape(2, 4, -1).astype(F32)
    qv_vector = jnp.take(qv_half, relative, axis=1)
    gains = small_all[1].transpose(2, 1, 3, 0, 4).reshape(2, D).astype(F32)
    biases = small_all[2].transpose(2, 1, 3, 0, 4).reshape(4, D).astype(F32)
    up_all = lax.dynamic_index_in_dim(small_all[3], tp_index, 1, False)
    up_vector = jnp.take(up_all.transpose(1, 0, 2).reshape(4, -1).astype(F32), relative, axis=0)

    kv_width = key_weight.shape[1] // 4
    heads_each = kv_width // DH
    heads_here = 4 * heads_each
    ff_half = up_weight.shape[1] // 8
    kv_own = collect(jnp.concatenate([own_columns(key_weight), own_columns(value_weight)], axis=1))
    query_own = collect(own_columns(query_weight))
    output_own = collect(own_columns(output_weight))
    up_piece = own_columns(up_weight)
    down_piece = own_columns(down_weight)
    up_own = [collect(up_piece[:, half * ff_half : (half + 1) * ff_half]) for half in range(2)]
    down_own = [collect(down_piece[:, half * ff_half : (half + 1) * ff_half]) for half in range(2)]
    key_value_w = spread(kv_own)
    query_w = spread(query_own)
    output_w = spread(output_own)

    tokens_two = jnp.concatenate([tokens, tokens_far], axis=0)
    zero_row = jnp.zeros((kv_width,), F32)
    kv_here = [
        (
            product(tokens_two, key_value_w[q]) + jnp.concatenate([zero_row, qv_vector[1, q]])
        ).astype(BF)
        for q in range(4)
    ]
    kv_near = [across(kv_here[q ^ 1], 1) for q in range(4)]
    queries = [(product(tokens, query_w[q]) + qv_vector[0, q]).astype(BF) for q in range(4)]
    attended, logsums = [], []
    for q in range(4):
        out, log = attention(queries[q], kv_here[q], kv_near[q])
        attended.append(out)
        logsums.append(log)
    attn_low = sum_products(attended, output_w)
    up_w = [spread(after(up_own[0], attended[1])), spread(after(up_own[1], attended[3]))]
    attn_branch = tp_sum(attn_low) + biases[0]
    normed_one, factor_one = normalize(tokens.astype(F32) + attn_branch)
    hidden_one = normed_one * gains[0] + biases[1]
    hidden_low = hidden_one.astype(BF)

    pairs = [(half, q) for half in range(2) for q in range(4)]
    up_rows = up_vector.reshape(4, 2, ff_half)
    pre_act = [product(hidden_low, up_w[half][q]) + up_rows[q, half] for half, q in pairs]
    activated = [gelu_tanh(item).astype(BF) for item in pre_act]
    down_w = [
        spread(after(down_own[0], activated[0])),
        spread(after(down_own[1], activated[4])),
    ]
    mlp_low = sum_products(activated, [down_w[half][q] for half, q in pairs])
    mlp_branch = tp_sum(mlp_low) + biases[2]
    second = hidden_one + mlp_branch
    normed_two, factor_two = normalize(second)
    result = normed_two * gains[1] + biases[3]
    grad_second = norm_backward(grad_out * gains[1], normed_two, factor_two)
    grad_mlp = grad_second.astype(BF)
    down_parts = [transposed_times(grad_mlp, item).astype(BF) for item in activated]
    down_grads = [reduce_columns(down_parts[half * 4 : half * 4 + 4]) for half in range(2)]
    grad_mlp_then = after(grad_mlp, *down_parts)
    grad_pre = []
    for at, (half, q) in enumerate(pairs):
        unused, gelu_pull = jax.vjp(gelu_tanh, pre_act[at])
        grad_pre.append(gelu_pull(product(grad_mlp_then, down_w[half][q]))[0].astype(BF))
    hidden_part = sum_products(grad_pre, [up_w[half][q] for half, q in pairs])
    grad_hidden = grad_second + tp_sum(hidden_part)
    up_parts = [transposed_times(hidden_low, item).astype(BF) for item in grad_pre]
    up_grads = [reduce_columns(up_parts[half * 4 : half * 4 + 4]) for half in range(2)]
    grad_first = norm_backward(grad_hidden * gains[0], normed_one, factor_one)
    grad_branch = grad_first.astype(BF)
    grad_attended = [product(grad_branch, output_w[q]).astype(BF) for q in range(4)]
    output_grads = reduce_columns(
        [transposed_times(grad_branch, attended[q]).astype(BF) for q in range(4)]
    )
    grad_q, here_sums, near_sums = [], [], []
    for q in range(4):
        dq, dk_here, dk_near, dv_here, dv_near = attention_back(
            queries[q], kv_here[q], kv_near[q], grad_attended[q], logsums[q]
        )
        grad_q.append(dq)
        here_sums.append((dk_here, dv_here))
        near_sums.append((across(dk_near, 1), across(dv_near, 1)))
    two_sums = [
        jnp.concatenate(
            [
                (here_sums[q][at].astype(F32) + near_sums[q ^ 1][at].astype(F32)).astype(BF)
                for at in range(2)
            ],
            axis=1,
        )
        for q in range(4)
    ]
    far_sums = [across(two_sums[q][local_rows:], 2) for q in range(4)]
    grad_kv = [
        (two_sums[q][:local_rows].astype(F32) + far_sums[q ^ 2].astype(F32)).astype(BF)
        for q in range(4)
    ]
    query_grads = reduce_columns([transposed_times(tokens, grad_q[q]).astype(BF) for q in range(4)])
    kv_grads = reduce_columns([transposed_times(tokens, grad_kv[q]).astype(BF) for q in range(4)])
    input_part = sum_products(grad_q + grad_kv, query_w + key_value_w)
    input_grad = grad_first + tp_sum(input_part)

    def canonical(rows):
        return jnp.take(jnp.stack(rows), relative, axis=0).reshape(-1)

    def column_sums(array):
        return jnp.sum(array.astype(F32), axis=0)

    pieces = [
        canonical([column_sums(grad_q[q]) for q in range(4)]),
        canonical([column_sums(grad_kv[q][:, kv_width:]) for q in range(4)]),
        canonical(
            [
                jnp.concatenate([column_sums(grad_pre[q]), column_sums(grad_pre[4 + q])])
                for q in range(4)
            ]
        ),
        jnp.sum(grad_hidden * normed_one, axis=0),
        jnp.sum(grad_out * normed_two, axis=0),
        column_sums(grad_branch),
        jnp.sum(grad_hidden, axis=0),
        column_sums(grad_mlp),
        jnp.sum(grad_out, axis=0),
        jnp.stack(
            [
                jnp.sum(second * second),
                jnp.sum(attn_branch * attn_branch),
                jnp.sum(mlp_branch * mlp_branch),
            ]
        ),
    ]
    sizes = [item.shape[0] for item in pieces]
    flat = jnp.concatenate(pieces + [jnp.zeros((-sum(sizes) % 1024,), F32)]).reshape(-1, 128)
    flat = butterfly(flat, ("ctx", "shard")).reshape(-1)
    totals = []
    at = 0
    for size in sizes:
        totals.append(flat[at : at + size])
        at += size
    shard_index = lax.axis_index("shard")
    piece = DH // n_shard
    heads_part = H // n_tp

    def last_piece(array, axis):
        return lax.dynamic_slice_in_dim(array, shard_index * piece, piece, axis)

    grad_qv_bias = last_piece(jnp.stack(totals[0:2]).reshape(2, heads_here, DH), 2)
    grad_up_bias = last_piece(totals[2].reshape(-1, DH), 1)

    def feature_rows(rows):
        stacked = jnp.stack(rows).reshape(len(rows), H, DH)
        return last_piece(
            lax.dynamic_slice_in_dim(stacked, tp_index * heads_part, heads_part, 1), 2
        )

    grad_gains = feature_rows(totals[3:5])
    grad_biases = feature_rows(totals[5:9])
    count_all = local_rows * n_shard * lax.axis_size("ctx") * D
    root_squares = jnp.sqrt(totals[9] / count_all)

    def whole(parts):
        return jnp.concatenate(ordered(parts, bits), axis=1).astype(F32)

    def whole_halves(parts):
        placed = [ordered(half, bits) for half in parts]
        return jnp.concatenate(
            [placed[half][q] for q in range(4) for half in range(2)], axis=1
        ).astype(F32)

    return (
        result.astype(BF).reshape(1, local_rows, D),
        input_grad.astype(BF).reshape(1, local_rows, D),
        whole(query_grads),
        whole([item[:, :kv_width] for item in kv_grads]),
        whole([item[:, kv_width:] for item in kv_grads]),
        whole(output_grads),
        whole_halves(up_grads),
        whole_halves(down_grads),
        grad_qv_bias,
        grad_up_bias,
        grad_gains,
        grad_biases,
        root_squares,
    )


def solution(mesh):
    if mesh.shape["ctx"] != 4 or mesh.shape["tp"] != 2:
        raise ValueError("unexpected mesh")
    placed = (
        P("shard", "ctx", None),
        P("shard", "ctx", None),
        P("shard", "tp"),
        P("shard", "tp"),
        P("shard", "tp"),
        P("shard", "tp"),
        P("shard", "tp"),
        P("shard", "tp"),
        P(None, "tp", "shard"),
        P("tp", "shard"),
        P(None, "tp", "shard"),
        P(None, "tp", "shard"),
    )
    return jax.shard_map(
        shards,
        mesh=mesh,
        in_specs=placed,
        out_specs=(
            P("shard", "ctx", None),
            P("shard", "ctx", None),
            P("shard", "tp"),
            P("shard", "tp"),
            P("shard", "tp"),
            P("shard", "tp"),
            P("shard", "tp"),
            P("shard", "tp"),
            P(None, "tp", "shard"),
            P("tp", "shard"),
            P(None, "tp", "shard"),
            P(None, "tp", "shard"),
            P(),
        ),
        check_vma=False,
    )
```

```python
import jax
import jax.numpy as jnp
from jax import lax
from jax.experimental import pallas as pl
from jax.experimental.pallas import tpu as pltpu
from jax.sharding import PartitionSpec as P

D = 2048
H = 16
DH = 128
SCALE = DH ** (-0.5)
BF = jnp.bfloat16
F32 = jnp.float32


epsilon = 1e-12


def product(left, right):
    return jnp.dot(left, right, preferred_element_type=F32)


def times_transposed(left, right):
    return lax.dot_general(left, right, (((1,), (1,)), ((), ())), preferred_element_type=F32)


def transposed_times(left, right):
    return lax.dot_general(left, right, (((0,), (0,)), ((), ())), preferred_element_type=F32)


def normalize(stream):
    center = stream - jnp.mean(stream, axis=-1, keepdims=True)
    factor = lax.rsqrt(jnp.mean(center * center, axis=-1, keepdims=True) + epsilon)
    return (center * factor, factor)


def norm_backward(grad_norm, normed, factor):
    return factor * (
        grad_norm
        - jnp.mean(grad_norm, axis=-1, keepdims=True)
        - normed * jnp.mean(grad_norm * normed, axis=-1, keepdims=True)
    )


def gelu_tanh(values):
    return jax.nn.gelu(values, approximate=True)


def contract(left, right, left_axis, right_axis):
    return lax.dot_general(
        left, right, (((left_axis,), (right_axis,)), ((), ())), preferred_element_type=F32
    )


def forward_kernel(q_ref, kh_ref, kn_ref, vh_ref, vn_ref, out_ref, log_ref):
    q = q_ref[...]
    near = contract(kh_ref[...], q, 1, 1) * SCALE
    far = contract(kn_ref[...], q, 1, 1) * SCALE
    peak = jnp.maximum(jnp.max(near, axis=0, keepdims=True), jnp.max(far, axis=0, keepdims=True))
    near = jnp.exp(near - peak)
    far = jnp.exp(far - peak)
    total = jnp.sum(near, axis=0, keepdims=True) + jnp.sum(far, axis=0, keepdims=True)
    out = contract(vh_ref[...], near.astype(BF), 0, 0) + contract(vn_ref[...], far.astype(BF), 0, 0)
    out_ref[...] = (out / total).T.astype(BF)
    log_ref[0] = peak + jnp.log(total)

def backward_kernel(q_ref, kh_ref, kn_ref, vh_ref, vn_ref, grad_ref, log_ref, dq_ref, dkh_ref, dkn_ref, dvh_ref, dvn_ref, *sums):
    step = pl.program_id(1)
    q = q_ref[...]
    grad = grad_ref[...]
    logsum = log_ref[0]
    probs, d_probs = [], []
    for k_ref, v_ref in ((kh_ref, vh_ref), (kn_ref, vn_ref)):
        probs.append(jnp.exp(contract(k_ref[...], q, 1, 1) * SCALE - logsum))
        d_probs.append(contract(v_ref[...], grad, 1, 1))
    inner = sum(jnp.sum(p * d, axis=0, keepdims=True) for p, d in zip(probs, d_probs))
    dq = 0.0
    for at, k_ref in enumerate((kh_ref, kn_ref)):
        d_scores = (probs[at] * (d_probs[at] - inner)).astype(BF)
        dq = dq + contract(k_ref[...], d_scores, 0, 0)
        dk = contract(d_scores, q, 1, 0)
        dv = contract(probs[at].astype(BF), grad, 1, 0)
        @pl.when(step == 0)
        def _():
            sums[at][...] = dk
            sums[2 + at][...] = dv
        @pl.when(step > 0)
        def _():
            sums[at][...] += dk
            sums[2 + at][...] += dv
    dq_ref[...] = (dq * SCALE).T.astype(BF)
    @pl.when(step == pl.num_programs(1) - 1)
    def _():
        dkh_ref[...] = (sums[0][...] * SCALE).astype(BF)
        dkn_ref[...] = (sums[1][...] * SCALE).astype(BF)
        dvh_ref[...] = sums[2][...].astype(BF)
        dvn_ref[...] = sums[3][...].astype(BF)

def kv_specs(rows, heads):
    k = pl.BlockSpec((rows, DH), lambda h, b: (0, h))
    v = pl.BlockSpec((rows, DH), lambda h, b: (0, heads + h))
    return k, k, v, v

def attention(q, kvh, kvn, block=None):
    rows, width = q.shape
    block = block or rows
    heads = width // DH
    row = pl.BlockSpec((block, DH), lambda h, b: (b, h))
    log = pl.BlockSpec((1, 1, block), lambda h, b: (h, 0, b))
    return pl.pallas_call(forward_kernel, grid=(heads, rows // block),
        in_specs=[row, *kv_specs(kvh.shape[0], heads)], out_specs=[row, log],
        out_shape=[jax.ShapeDtypeStruct((rows, width), BF), jax.ShapeDtypeStruct((heads, 1, rows), F32)],
        name="attention_forward")(q, kvh, kvn, kvh, kvn)

def attention_back(q, kvh, kvn, grad, logsum, block=None):
    rows, width = q.shape
    block = block or rows
    heads = width // DH
    keys = kvh.shape[0]
    row = pl.BlockSpec((block, DH), lambda h, b: (b, h))
    log = pl.BlockSpec((1, 1, block), lambda h, b: (h, 0, b))
    k = pl.BlockSpec((keys, DH), lambda h, b: (0, h))
    return pl.pallas_call(backward_kernel, grid=(heads, rows // block),
        in_specs=[row, *kv_specs(keys, heads), row, log],
        out_specs=[row, k, k, k, k],
        out_shape=[jax.ShapeDtypeStruct((rows, width), BF)] + [jax.ShapeDtypeStruct((keys, width), BF)] * 4,
        scratch_shapes=[pltpu.VMEM((keys, DH), F32)] * 4,
        name="attention_backward")(q, kvh, kvn, kvh, kvn, grad, logsum)


def sum_kernel(*refs):
    count = (len(refs) - 1) // 2
    total = 0.0
    for at in range(count):
        total = total + contract(refs[at][...], refs[count + at][...], 1, 1)
    refs[-1][...] = total.astype(refs[-1].dtype)


def sum_products(lefts, rights, block=256):
    rows = lefts[0].shape[0]
    width = rights[0].shape[0]
    return pl.pallas_call(
        sum_kernel,
        grid=(width // block,),
        in_specs=[pl.BlockSpec(left.shape, lambda n: (0, 0)) for left in lefts]
        + [pl.BlockSpec((block, right.shape[1]), lambda n: (n, 0)) for right in rights],
        out_specs=pl.BlockSpec((rows, block), lambda n: (0, n)),
        out_shape=jax.ShapeDtypeStruct((rows, width), BF),
        name="sum_products",
    )(*lefts, *rights)


def after(value, *others):
    return lax.optimization_barrier((value,) + others)[0]


def across(array, step, axis="ctx"):
    size = lax.axis_size(axis)
    return lax.ppermute(array, axis, [(at, at ^ step) for at in range(size)])


def collect(piece):
    return lax.all_gather(piece, "shard", axis=0, tiled=True)


def scatter(total):
    return lax.psum_scatter(total, "shard", scatter_dimension=0, tiled=True)


def scatter_direct(total):
    size = lax.axis_size("shard")
    rows = total.shape[0] // size
    index = lax.axis_index("shard")

    def block(step):
        return lax.dynamic_slice_in_dim(total, ((index + step) % size) * rows, rows, 0)

    got = [
        lax.ppermute(block(step), "shard", [(at, (at + step) % size) for at in range(size)])
        for step in range(1, size)
    ]
    return block(0), got


def sum_direct(mine, got):
    return sum([item.astype(F32) for item in got], mine.astype(F32)).astype(BF)


def fill(own, far):
    return [own, across(own, 1), far, across(far, 1)]


def spread(own):
    return fill(own, across(own, 2))


def near_sums(parts):
    return [
        (parts[q].astype(F32) + across(parts[q + 1], 1).astype(F32)).astype(BF) for q in (0, 2)
    ]


def reduce_pair(parts):
    return far_sum(*near_sums(parts))


def far_sum(own, far):
    return (own.astype(F32) + across(far, 2).astype(F32)).astype(BF)


def join_pair(own, far):
    return fill(far_sum(own, far), far_sum(far, own))


def ordered(pieces, bits):
    low, high = bits
    swapped = [jnp.where(high, pieces[q ^ 2], pieces[q]) for q in range(4)]
    return [jnp.where(low, swapped[q ^ 1], swapped[q]) for q in range(4)]


def tp_sum(low):
    return low.astype(F32) + across(low, 1, "tp").astype(F32)


def butterfly(flat, axes):
    for axis in axes:
        step = 1
        while step < lax.axis_size(axis):
            flat = flat + across(flat, step, axis)
            step *= 2
    return flat


def shards(
    inputs,
    cotangent,
    query_weight,
    key_weight,
    value_weight,
    output_weight,
    up_weight,
    down_weight,
    query_value_bias,
    up_bias,
    norm_gains,
    other_biases,
):
    local_rows = inputs.shape[1]
    member = lax.axis_index("ctx")
    relative = jnp.arange(4) ^ member
    bits = ((member & 1) == 1, (member & 2) == 2)
    n_shard = lax.axis_size("shard")
    n_tp = lax.axis_size("tp")

    def own_columns(weight):
        width = weight.shape[1] // 4
        return lax.dynamic_slice_in_dim(weight, member * width, width, 1)

    tokens = inputs.reshape(local_rows, D)
    tokens_far = across(tokens, 2)
    grad_out = cotangent.reshape(local_rows, D).astype(F32)

    small = (query_value_bias, norm_gains, other_biases, up_bias)
    packed = jnp.concatenate([item.reshape(1, -1) for item in small], axis=1)
    tp_index = lax.axis_index("tp")
    slot = lax.axis_index("shard") * n_tp + tp_index
    packed_all = lax.dynamic_update_slice_in_dim(
        jnp.zeros((n_shard * n_tp, packed.shape[1]), BF), packed, slot, 0
    )
    packed_all = butterfly(packed_all, ("tp", "shard"))
    packed_all = packed_all.reshape(n_shard, n_tp, packed.shape[1])
    at = 0
    small_all = []
    for item in small:
        part = packed_all[:, :, at : at + item.size].reshape((n_shard, n_tp) + item.shape)
        at += item.size
        small_all.append(part)
    qv_all = lax.dynamic_index_in_dim(small_all[0], tp_index, 1, False)
    qv_half = qv_all.transpose(1, 2, 0, 3).reshape(2, 4, -1).astype(F32)
    qv_vector = jnp.take(qv_half, relative, axis=1)
    gains = small_all[1].transpose(2, 1, 3, 0, 4).reshape(2, D).astype(F32)
    biases = small_all[2].transpose(2, 1, 3, 0, 4).reshape(4, D).astype(F32)
    up_all = lax.dynamic_index_in_dim(small_all[3], tp_index, 1, False)
    up_vector = jnp.take(up_all.transpose(1, 0, 2).reshape(4, -1).astype(F32), relative, axis=0)

    kv_width = key_weight.shape[1] // 4
    heads_each = kv_width // DH
    heads_here = 4 * heads_each
    ff_half = up_weight.shape[1] // 8
    kv_own = collect(jnp.concatenate([own_columns(key_weight), own_columns(value_weight)], axis=1))
    query_own = collect(own_columns(query_weight))
    output_own = collect(own_columns(output_weight))
    up_piece = own_columns(up_weight)
    down_piece = own_columns(down_weight)
    up_own = [collect(up_piece[:, half * ff_half : (half + 1) * ff_half]) for half in range(2)]
    down_own = [collect(down_piece[:, half * ff_half : (half + 1) * ff_half]) for half in range(2)]
    key_value_w = fill(kv_own, across(after(kv_own, tokens_far), 2))
    query_w = spread(query_own)

    tokens_two = jnp.concatenate([tokens, tokens_far], axis=0)
    zero_row = jnp.zeros((kv_width,), F32)
    kv_here = [
        (
            product(tokens_two, key_value_w[q]) + jnp.concatenate([zero_row, qv_vector[1, q]])
        ).astype(BF)
        for q in range(4)
    ]
    output_w = spread(after(output_own, kv_here[3]))
    kv_near = [across(kv_here[q ^ 1], 1) for q in range(4)]
    queries = [(product(tokens, query_w[q]) + qv_vector[0, q]).astype(BF) for q in range(4)]
    attended, logsums = [], []
    for q in range(4):
        out, log = attention(queries[q], kv_here[q], kv_near[q])
        attended.append(out)
        logsums.append(log)
    attn_low = sum_products(attended, output_w)
    up_w = [spread(up_own[0]), spread(after(up_own[1], attended[3]))]
    attn_branch = tp_sum(attn_low) + biases[0]
    normed_one, factor_one = normalize(tokens.astype(F32) + attn_branch)
    hidden_one = normed_one * gains[0] + biases[1]
    hidden_low = hidden_one.astype(BF)

    pairs = [(half, q) for half in range(2) for q in range(4)]
    up_rows = up_vector.reshape(4, 2, ff_half)
    pre_act = [product(hidden_low, up_w[half][q]) + up_rows[q, half] for half, q in pairs]
    activated = [gelu_tanh(item).astype(BF) for item in pre_act]
    down_w = [
        spread(after(down_own[0], activated[0])),
        spread(after(down_own[1], activated[4])),
    ]
    mlp_low = sum_products(activated, [down_w[half][q] for half, q in pairs])
    mlp_branch = tp_sum(mlp_low) + biases[2]
    second = hidden_one + mlp_branch
    normed_two, factor_two = normalize(second)
    result = normed_two * gains[1] + biases[3]
    grad_second = norm_backward(grad_out * gains[1], normed_two, factor_two)
    grad_mlp = grad_second.astype(BF)
    down_parts = [transposed_times(grad_mlp, item).astype(BF) for item in activated]
    down_late = near_sums(down_parts[4:8])
    down_early = near_sums(down_parts[0:4])
    grad_mlp_then = after(grad_mlp, *down_late, *down_early)
    down_second = [scatter(item) for item in down_late]
    down_first = scatter(far_sum(*down_early))
    grad_pre = []
    for at, (half, q) in enumerate(pairs):
        unused, gelu_pull = jax.vjp(gelu_tanh, pre_act[at])
        grad_pre.append(gelu_pull(product(grad_mlp_then, down_w[half][q]))[0].astype(BF))
    hidden_part = sum_products(grad_pre, [up_w[half][q] for half, q in pairs])
    grad_hidden = grad_second + tp_sum(hidden_part)
    up_parts = [transposed_times(hidden_low, item).astype(BF) for item in grad_pre]
    up_late = near_sums(up_parts[4:8])
    up_second = [scatter(item) for item in up_late]
    up_total = reduce_pair(up_parts[0:4])
    up_first = scatter(up_total)
    grad_first = norm_backward(grad_hidden * gains[0], normed_one, factor_one)
    grad_branch = grad_first.astype(BF)
    grad_attended = [product(grad_branch, output_w[q]).astype(BF) for q in range(4)]
    output_direct = scatter_direct(
        reduce_pair([transposed_times(grad_branch, attended[q]).astype(BF) for q in range(4)])
    )
    grad_attended[2:] = lax.optimization_barrier((*grad_attended[2:], up_total))[:-1]
    grad_q, here_parts, near_parts = [], [], []
    for q in range(4):
        dq, dk_here, dk_near, dv_here, dv_near = attention_back(
            queries[q], kv_here[q], kv_near[q], grad_attended[q], logsums[q]
        )
        grad_q.append(dq)
        here_parts.append((dk_here, dv_here))
        near_parts.append((across(dk_near, 1), across(dv_near, 1)))
    two_sums = [
        jnp.concatenate(
            [
                (here_parts[q][at].astype(F32) + near_parts[q ^ 1][at].astype(F32)).astype(BF)
                for at in range(2)
            ],
            axis=1,
        )
        for q in range(4)
    ]
    far_sums = [across(two_sums[q][local_rows:], 2) for q in range(4)]
    grad_kv = [
        (two_sums[q][:local_rows].astype(F32) + far_sums[q ^ 2].astype(F32)).astype(BF)
        for q in range(4)
    ]
    query_direct = scatter_direct(
        reduce_pair([transposed_times(tokens, grad_q[q]).astype(BF) for q in range(4)])
    )
    kv_total = reduce_pair([transposed_times(tokens, grad_kv[q]).astype(BF) for q in range(4)])
    kv_mine = scatter(kv_total)
    query_mine, query_got = lax.optimization_barrier((*query_direct, kv_total))[:2]
    output_mine, output_got = lax.optimization_barrier((*output_direct, kv_total))[:2]
    down_first, up_first, grad_q_then = (
        after(item, kv_total) for item in (down_first, up_first, grad_q[0])
    )
    down_second = [after(item, kv_total) for item in down_second]
    up_second = [after(item, kv_total) for item in up_second]
    down_grads = [spread(down_first), join_pair(*down_second)]
    up_grads = [spread(up_first), join_pair(*up_second)]
    output_grads = spread(sum_direct(output_mine, output_got))
    query_grads = spread(sum_direct(query_mine, query_got))
    kv_grads = spread(kv_mine)
    input_part = sum_products([grad_q_then] + grad_q[1:] + grad_kv, query_w + key_value_w)
    input_grad = grad_first + tp_sum(input_part)

    def canonical(rows):
        return jnp.take(jnp.stack(rows), relative, axis=0).reshape(-1)

    def column_sums(array):
        return jnp.sum(array.astype(F32), axis=0)

    pieces = [
        canonical([column_sums(grad_q[q]) for q in range(4)]),
        canonical([column_sums(grad_kv[q][:, kv_width:]) for q in range(4)]),
        canonical(
            [
                jnp.concatenate([column_sums(grad_pre[q]), column_sums(grad_pre[4 + q])])
                for q in range(4)
            ]
        ),
        jnp.sum(grad_hidden * normed_one, axis=0),
        jnp.sum(grad_out * normed_two, axis=0),
        column_sums(grad_branch),
        jnp.sum(grad_hidden, axis=0),
        column_sums(grad_mlp),
        jnp.sum(grad_out, axis=0),
        jnp.stack(
            [
                jnp.sum(second * second),
                jnp.sum(attn_branch * attn_branch),
                jnp.sum(mlp_branch * mlp_branch),
            ]
        ),
    ]
    sizes = [item.shape[0] for item in pieces]
    flat = jnp.concatenate(pieces + [jnp.zeros((-sum(sizes) % 1024,), F32)]).reshape(-1, 128)
    flat = butterfly(after(flat, kv_total), ("ctx", "shard")).reshape(-1)
    totals = []
    at = 0
    for size in sizes:
        totals.append(flat[at : at + size])
        at += size
    shard_index = lax.axis_index("shard")
    piece = DH // n_shard
    heads_part = H // n_tp

    def last_piece(array, axis):
        return lax.dynamic_slice_in_dim(array, shard_index * piece, piece, axis)

    grad_qv_bias = last_piece(jnp.stack(totals[0:2]).reshape(2, heads_here, DH), 2)
    grad_up_bias = last_piece(totals[2].reshape(-1, DH), 1)

    def feature_rows(rows):
        stacked = jnp.stack(rows).reshape(len(rows), H, DH)
        return last_piece(
            lax.dynamic_slice_in_dim(stacked, tp_index * heads_part, heads_part, 1), 2
        )

    grad_gains = feature_rows(totals[3:5])
    grad_biases = feature_rows(totals[5:9])
    count_all = local_rows * n_shard * lax.axis_size("ctx") * D
    root_squares = jnp.sqrt(totals[9] / count_all)

    def whole(parts):
        return jnp.concatenate(ordered(parts, bits), axis=1).astype(F32)

    def whole_halves(parts):
        placed = [ordered(half, bits) for half in parts]
        return jnp.concatenate(
            [placed[half][q] for q in range(4) for half in range(2)], axis=1
        ).astype(F32)

    return (
        result.astype(BF).reshape(1, local_rows, D),
        input_grad.astype(BF).reshape(1, local_rows, D),
        whole(query_grads),
        whole([item[:, :kv_width] for item in kv_grads]),
        whole([item[:, kv_width:] for item in kv_grads]),
        whole(output_grads),
        whole_halves(up_grads),
        whole_halves(down_grads),
        grad_qv_bias,
        grad_up_bias,
        grad_gains,
        grad_biases,
        root_squares,
    )


def solution(mesh):
    if mesh.shape["ctx"] != 4 or mesh.shape["tp"] != 2:
        raise ValueError("unexpected mesh")
    placed = (
        P("shard", "ctx", None),
        P("shard", "ctx", None),
        P("shard", "tp"),
        P("shard", "tp"),
        P("shard", "tp"),
        P("shard", "tp"),
        P("shard", "tp"),
        P("shard", "tp"),
        P(None, "tp", "shard"),
        P("tp", "shard"),
        P(None, "tp", "shard"),
        P(None, "tp", "shard"),
    )
    return jax.shard_map(
        shards,
        mesh=mesh,
        in_specs=placed,
        out_specs=(
            P("shard", "ctx", None),
            P("shard", "ctx", None),
            P("shard", "tp"),
            P("shard", "tp"),
            P("shard", "tp"),
            P("shard", "tp"),
            P("shard", "tp"),
            P("shard", "tp"),
            P(None, "tp", "shard"),
            P("tp", "shard"),
            P(None, "tp", "shard"),
            P(None, "tp", "shard"),
            P(),
        ),
        check_vma=False,
    )
```

```python
import jax
import jax.numpy as jnp
from jax import lax
from jax.experimental import pallas as pl
from jax.experimental.pallas import tpu as pltpu
from jax.sharding import PartitionSpec as P


D = 2048
H = 16
DH = 128
SCALE = DH ** (-0.5)
BF = jnp.bfloat16
F32 = jnp.float32


epsilon = 1e-12


def product(left, right):
    return jnp.dot(left, right, preferred_element_type=F32)


def transposed_times(left, right):
    return lax.dot_general(left, right, (((0,), (0,)), ((), ())), preferred_element_type=F32)


def normalize(stream):
    center = stream - jnp.mean(stream, axis=-1, keepdims=True)
    factor = lax.rsqrt(jnp.mean(center * center, axis=-1, keepdims=True) + epsilon)
    return (center * factor, factor)


def norm_backward(grad_norm, normed, factor):
    return factor * (
        grad_norm
        - jnp.mean(grad_norm, axis=-1, keepdims=True)
        - normed * jnp.mean(grad_norm * normed, axis=-1, keepdims=True)
    )


def gelu_tanh(values):
    return jax.nn.gelu(values, approximate=True)


def contract(left, right, left_axis, right_axis):
    return lax.dot_general(
        left, right, (((left_axis,), (right_axis,)), ((), ())), preferred_element_type=F32
    )


def forward_kernel(q_ref, kh_ref, kn_ref, vh_ref, vn_ref, out_ref, log_ref):
    q = q_ref[...]
    near = contract(kh_ref[...], q, 1, 1) * SCALE
    far = contract(kn_ref[...], q, 1, 1) * SCALE
    peak = jnp.maximum(jnp.max(near, axis=0, keepdims=True), jnp.max(far, axis=0, keepdims=True))
    near = jnp.exp(near - peak)
    far = jnp.exp(far - peak)
    total = jnp.sum(near, axis=0, keepdims=True) + jnp.sum(far, axis=0, keepdims=True)
    out = contract(vh_ref[...], near.astype(BF), 0, 0) + contract(vn_ref[...], far.astype(BF), 0, 0)
    out_ref[...] = (out / total).T.astype(BF)
    log_ref[0] = peak + jnp.log(total)


def backward_kernel(q_ref, kh_ref, kn_ref, vh_ref, vn_ref, grad_ref, log_ref, dq_ref, dkh_ref, dkn_ref, dvh_ref, dvn_ref, *sums):
    step = pl.program_id(1)
    q = q_ref[...]
    grad = grad_ref[...]
    logsum = log_ref[0]
    probs, d_probs = [], []
    for k_ref, v_ref in ((kh_ref, vh_ref), (kn_ref, vn_ref)):
        probs.append(jnp.exp(contract(k_ref[...], q, 1, 1) * SCALE - logsum))
        d_probs.append(contract(v_ref[...], grad, 1, 1))
    inner = sum(jnp.sum(p * d, axis=0, keepdims=True) for p, d in zip(probs, d_probs))
    dq = 0.0
    for at, k_ref in enumerate((kh_ref, kn_ref)):
        d_scores = (probs[at] * (d_probs[at] - inner)).astype(BF)
        dq = dq + contract(k_ref[...], d_scores, 0, 0)
        dk = contract(d_scores, q, 1, 0)
        dv = contract(probs[at].astype(BF), grad, 1, 0)

        @pl.when(step == 0)
        def _():
            sums[at][...] = dk
            sums[2 + at][...] = dv

        @pl.when(step > 0)
        def _():
            sums[at][...] += dk
            sums[2 + at][...] += dv
    dq_ref[...] = (dq * SCALE).T.astype(BF)

    @pl.when(step == pl.num_programs(1) - 1)
    def _():
        dkh_ref[...] = (sums[0][...] * SCALE).astype(BF)
        dkn_ref[...] = (sums[1][...] * SCALE).astype(BF)
        dvh_ref[...] = sums[2][...].astype(BF)
        dvn_ref[...] = sums[3][...].astype(BF)


def kv_specs(rows, heads):
    k = pl.BlockSpec((rows, DH), lambda h, b: (0, h))
    v = pl.BlockSpec((rows, DH), lambda h, b: (0, heads + h))
    return k, k, v, v


def attention(q, kvh, kvn, block=None):
    rows, width = q.shape
    block = block or rows
    heads = width // DH
    row = pl.BlockSpec((block, DH), lambda h, b: (b, h))
    log = pl.BlockSpec((1, 1, block), lambda h, b: (h, 0, b))
    return pl.pallas_call(forward_kernel, grid=(heads, rows // block),
        in_specs=[row, *kv_specs(kvh.shape[0], heads)], out_specs=[row, log],
        out_shape=[jax.ShapeDtypeStruct((rows, width), BF), jax.ShapeDtypeStruct((heads, 1, rows), F32)],
        name="attention_forward")(q, kvh, kvn, kvh, kvn)


def attention_back(q, kvh, kvn, grad, logsum, block=None):
    rows, width = q.shape
    block = block or rows
    heads = width // DH
    keys = kvh.shape[0]
    row = pl.BlockSpec((block, DH), lambda h, b: (b, h))
    log = pl.BlockSpec((1, 1, block), lambda h, b: (h, 0, b))
    k = pl.BlockSpec((keys, DH), lambda h, b: (0, h))
    return pl.pallas_call(backward_kernel, grid=(heads, rows // block),
        in_specs=[row, *kv_specs(keys, heads), row, log],
        out_specs=[row, k, k, k, k],
        out_shape=[jax.ShapeDtypeStruct((rows, width), BF)] + [jax.ShapeDtypeStruct((keys, width), BF)] * 4,
        scratch_shapes=[pltpu.VMEM((keys, DH), F32)] * 4,
        name="attention_backward")(q, kvh, kvn, kvh, kvn, grad, logsum)


def sum_kernel(*refs):
    count = (len(refs) - 1) // 2
    total = 0.0
    for at in range(count):
        total = total + contract(refs[at][...], refs[count + at][...], 1, 1)
    refs[-1][...] = total.astype(refs[-1].dtype)


def sum_products(lefts, rights, block=256):
    rows = lefts[0].shape[0]
    width = rights[0].shape[0]
    return pl.pallas_call(
        sum_kernel,
        grid=(width // block,),
        in_specs=[pl.BlockSpec(left.shape, lambda n: (0, 0)) for left in lefts]
        + [pl.BlockSpec((block, right.shape[1]), lambda n: (n, 0)) for right in rights],
        out_specs=pl.BlockSpec((rows, block), lambda n: (0, n)),
        out_shape=jax.ShapeDtypeStruct((rows, width), BF),
        name="sum_products",
    )(*lefts, *rights)


def after(value, *others):
    return lax.optimization_barrier((value,) + others)[0]


def across(array, step, axis="ctx"):
    size = lax.axis_size(axis)
    return lax.ppermute(array, axis, [(at, at ^ step) for at in range(size)])


def collect(piece):
    return lax.all_gather(piece, "shard", axis=0, tiled=True)


def scatter(total):
    return lax.psum_scatter(total, "shard", scatter_dimension=0, tiled=True)


def scatter_direct(total):
    size = lax.axis_size("shard")
    rows = total.shape[0] // size
    index = lax.axis_index("shard")

    def block(step):
        return lax.dynamic_slice_in_dim(total, ((index + step) % size) * rows, rows, 0)

    got = [
        lax.ppermute(block(step), "shard", [(at, (at + step) % size) for at in range(size)])
        for step in range(1, size)
    ]
    return block(0), got


def sum_direct(mine, got):
    return sum([item.astype(F32) for item in got], mine.astype(F32)).astype(BF)


def fill(own, far):
    return [own, across(own, 1), far, across(far, 1)]


def spread(own):
    return fill(own, across(own, 2))


def near_sums(parts):
    return [
        (parts[q].astype(F32) + across(parts[q + 1], 1).astype(F32)).astype(BF) for q in (0, 2)
    ]


def far_sum(own, far, *hold):
    got = across(far, 2)
    if hold:
        got = after(got, *hold)
    return (own.astype(F32) + got.astype(F32)).astype(BF)


def join_pair(own, far):
    return fill(far_sum(own, far), far_sum(far, own))


def ordered(pieces, bits):
    low, high = bits
    swapped = [jnp.where(high, pieces[q ^ 2], pieces[q]) for q in range(4)]
    return [jnp.where(low, swapped[q ^ 1], swapped[q]) for q in range(4)]


def tp_sum(low):
    return low.astype(F32) + across(low, 1, "tp").astype(F32)


def butterfly(flat, axes):
    for axis in axes:
        step = 1
        while step < lax.axis_size(axis):
            flat = flat + across(flat, step, axis)
            step *= 2
    return flat


def shards(
    inputs,
    cotangent,
    query_weight,
    key_weight,
    value_weight,
    output_weight,
    up_weight,
    down_weight,
    query_value_bias,
    up_bias,
    norm_gains,
    other_biases,
):
    local_rows = inputs.shape[1]
    member = lax.axis_index("ctx")
    relative = jnp.arange(4) ^ member
    bits = ((member & 1) == 1, (member & 2) == 2)
    n_shard = lax.axis_size("shard")
    n_tp = lax.axis_size("tp")

    def own_columns(weight, step=0):
        width = weight.shape[1] // 4
        return lax.dynamic_slice_in_dim(weight, (member ^ step) * width, width, 1)

    tokens = inputs.reshape(local_rows, D)
    tokens_far = across(tokens, 2)
    grad_out = cotangent.reshape(local_rows, D).astype(F32)

    small = (query_value_bias, norm_gains, other_biases, up_bias)
    packed = jnp.concatenate([item.reshape(1, -1) for item in small], axis=1)
    tp_index = lax.axis_index("tp")
    slot = lax.axis_index("shard") * n_tp + tp_index
    packed_all = lax.dynamic_update_slice_in_dim(
        jnp.zeros((n_shard * n_tp, packed.shape[1]), BF), packed, slot, 0
    )
    packed_all = butterfly(packed_all, ("tp", "shard"))
    packed_all = packed_all.reshape(n_shard, n_tp, packed.shape[1])
    at = 0
    small_all = []
    for item in small:
        part = packed_all[:, :, at : at + item.size].reshape((n_shard, n_tp) + item.shape)
        at += item.size
        small_all.append(part)
    qv_all = lax.dynamic_index_in_dim(small_all[0], tp_index, 1, False)
    qv_half = qv_all.transpose(1, 2, 0, 3).reshape(2, 4, -1).astype(F32)
    qv_vector = jnp.take(qv_half, relative, axis=1)
    gains = small_all[1].transpose(2, 1, 3, 0, 4).reshape(2, D).astype(F32)
    biases = small_all[2].transpose(2, 1, 3, 0, 4).reshape(4, D).astype(F32)
    up_all = lax.dynamic_index_in_dim(small_all[3], tp_index, 1, False)
    up_vector = jnp.take(up_all.transpose(1, 0, 2).reshape(4, -1).astype(F32), relative, axis=0)

    kv_width = key_weight.shape[1] // 4
    heads_each = kv_width // DH
    heads_here = 4 * heads_each
    ff_half = up_weight.shape[1] // 8
    kv_own = collect(jnp.concatenate([own_columns(key_weight), own_columns(value_weight)], axis=1))
    query_own = collect(own_columns(query_weight))
    output_own = collect(own_columns(output_weight))
    up_piece = own_columns(up_weight)
    down_piece = own_columns(down_weight)
    up_own = [collect(up_piece[:, half * ff_half : (half + 1) * ff_half]) for half in range(2)]
    down_own = [collect(down_piece[:, half * ff_half : (half + 1) * ff_half]) for half in range(2)]
    down_far = collect(own_columns(down_weight, 2)[:, ff_half:])
    key_value_w = fill(kv_own, across(after(kv_own, tokens_far), 2))
    query_w = spread(query_own)

    tokens_two = jnp.concatenate([tokens, tokens_far], axis=0)
    zero_row = jnp.zeros((kv_width,), F32)
    kv_here = [
        (
            product(tokens_two, key_value_w[q]) + jnp.concatenate([zero_row, qv_vector[1, q]])
        ).astype(BF)
        for q in range(4)
    ]
    output_w = spread(after(output_own, kv_here[3]))
    kv_near = [across(kv_here[q ^ 1], 1) for q in range(4)]
    queries = [(product(tokens, query_w[q]) + qv_vector[0, q]).astype(BF) for q in range(4)]
    attended, logsums = [], []
    for q in range(4):
        out, log = attention(queries[q], kv_here[q], kv_near[q])
        attended.append(out)
        logsums.append(log)
    attn_low = sum_products(attended, output_w)
    up_far = across(up_own[0], 2)
    up_w = [fill(up_own[0], up_far), spread(after(up_own[1], attended[3]))]
    attn_branch = tp_sum(attn_low) + biases[0]
    normed_one, factor_one = normalize(tokens.astype(F32) + attn_branch)
    hidden_one = normed_one * gains[0] + biases[1]
    hidden_low = hidden_one.astype(BF)

    pairs = [(half, q) for half in range(2) for q in range(4)]
    up_rows = up_vector.reshape(4, 2, ff_half)
    pre_act = [product(hidden_low, up_w[half][q]) + up_rows[q, half] for half, q in pairs]
    activated = [gelu_tanh(item).astype(BF) for item in pre_act]
    down_w = [
        spread(after(down_own[0], activated[0])),
        fill(down_own[1], down_far),
    ]
    mlp_low = sum_products(activated, [down_w[half][q] for half, q in pairs])
    mlp_branch = tp_sum(mlp_low) + biases[2]
    second = hidden_one + mlp_branch
    normed_two, factor_two = normalize(second)
    result = normed_two * gains[1] + biases[3]
    grad_second = norm_backward(grad_out * gains[1], normed_two, factor_two)
    grad_mlp = grad_second.astype(BF)
    down_parts = [transposed_times(grad_mlp, item).astype(BF) for item in activated]
    down_late = near_sums(down_parts[4:8])
    down_early = near_sums(down_parts[0:4])
    grad_mlp_then = after(grad_mlp, *down_late, *down_early)
    down_second = [scatter(item) for item in down_late]
    grad_pre = []
    for at, (half, q) in enumerate(pairs):
        _, gelu_pull = jax.vjp(gelu_tanh, pre_act[at])
        grad_pre.append(gelu_pull(product(grad_mlp_then, down_w[half][q]))[0].astype(BF))
    hidden_part = sum_products(grad_pre, [up_w[half][q] for half, q in pairs])
    down_first = scatter(far_sum(*down_early, hidden_part))
    grad_hidden = grad_second + tp_sum(hidden_part)
    up_parts = [transposed_times(hidden_low, item).astype(BF) for item in grad_pre]
    up_late = near_sums(up_parts[4:8])
    up_second = [scatter(item) for item in up_late]
    up_early = near_sums(up_parts[0:4])
    grad_first = norm_backward(grad_hidden * gains[0], normed_one, factor_one)
    grad_branch = grad_first.astype(BF)
    grad_attended = [product(grad_branch, output_w[q]).astype(BF) for q in range(4)]
    up_total = far_sum(*up_early, grad_branch)
    up_first = scatter(up_total)
    output_early = near_sums(
        [transposed_times(grad_branch, attended[q]).astype(BF) for q in range(4)]
    )
    grad_attended[2:] = lax.optimization_barrier((*grad_attended[2:], up_total))[:-1]
    grad_q, here_parts, near_parts = [], [], []
    for q in range(4):
        dq, dk_here, dk_near, dv_here, dv_near = attention_back(
            queries[q], kv_here[q], kv_near[q], grad_attended[q], logsums[q]
        )
        grad_q.append(dq)
        here_parts.append((dk_here, dv_here))
        near_parts.append((across(dk_near, 1), across(dv_near, 1)))
    two_sums = [
        jnp.concatenate(
            [
                (here_parts[q][at].astype(F32) + near_parts[q ^ 1][at].astype(F32)).astype(BF)
                for at in range(2)
            ],
            axis=1,
        )
        for q in range(4)
    ]
    far_sums = [across(two_sums[q][local_rows:], 2) for q in range(4)]
    grad_kv = [
        (two_sums[q][:local_rows].astype(F32) + far_sums[q ^ 2].astype(F32)).astype(BF)
        for q in range(4)
    ]
    output_direct = scatter_direct(far_sum(*output_early, *grad_q))
    query_early = near_sums([transposed_times(tokens, grad_q[q]).astype(BF) for q in range(4)])
    kv_total = far_sum(
        *near_sums([transposed_times(tokens, grad_kv[q]).astype(BF) for q in range(4)])
    )
    kv_mine = scatter(kv_total)
    query_mine, query_got = scatter_direct(far_sum(*query_early, kv_total))
    output_mine, output_got = lax.optimization_barrier((*output_direct, kv_total))[:2]
    down_first, up_first, grad_q_then = (
        after(item, kv_total) for item in (down_first, up_first, grad_q[0])
    )
    down_second = [after(item, kv_total) for item in down_second]
    up_second = [after(item, kv_total) for item in up_second]
    down_grads = [spread(down_first), join_pair(*down_second)]
    up_grads = [spread(up_first), join_pair(*up_second)]
    output_grads = spread(sum_direct(output_mine, output_got))
    query_grads = spread(sum_direct(query_mine, query_got))
    kv_grads = spread(kv_mine)
    input_part = sum_products([grad_q_then] + grad_q[1:] + grad_kv, query_w + key_value_w)
    input_grad = grad_first + tp_sum(input_part)

    def canonical(rows):
        return jnp.take(jnp.stack(rows), relative, axis=0).reshape(-1)

    def column_sums(array):
        return jnp.sum(array.astype(F32), axis=0)

    pieces = [
        canonical([column_sums(grad_q[q]) for q in range(4)]),
        canonical([column_sums(grad_kv[q][:, kv_width:]) for q in range(4)]),
        canonical(
            [
                jnp.concatenate([column_sums(grad_pre[q]), column_sums(grad_pre[4 + q])])
                for q in range(4)
            ]
        ),
        jnp.sum(grad_hidden * normed_one, axis=0),
        jnp.sum(grad_out * normed_two, axis=0),
        column_sums(grad_branch),
        jnp.sum(grad_hidden, axis=0),
        column_sums(grad_mlp),
        jnp.sum(grad_out, axis=0),
        jnp.stack(
            [
                jnp.sum(second * second),
                jnp.sum(attn_branch * attn_branch),
                jnp.sum(mlp_branch * mlp_branch),
            ]
        ),
    ]
    sizes = [item.shape[0] for item in pieces]
    flat = jnp.concatenate(pieces + [jnp.zeros((-sum(sizes) % 1024,), F32)]).reshape(-1, 128)
    flat = butterfly(after(flat, kv_total), ("ctx", "shard")).reshape(-1)
    totals = []
    at = 0
    for size in sizes:
        totals.append(flat[at : at + size])
        at += size
    shard_index = lax.axis_index("shard")
    piece = DH // n_shard
    heads_part = H // n_tp

    def last_piece(array, axis):
        return lax.dynamic_slice_in_dim(array, shard_index * piece, piece, axis)

    grad_qv_bias = last_piece(jnp.stack(totals[0:2]).reshape(2, heads_here, DH), 2)
    grad_up_bias = last_piece(totals[2].reshape(-1, DH), 1)

    def feature_rows(rows):
        stacked = jnp.stack(rows).reshape(len(rows), H, DH)
        return last_piece(
            lax.dynamic_slice_in_dim(stacked, tp_index * heads_part, heads_part, 1), 2
        )

    grad_gains = feature_rows(totals[3:5])
    grad_biases = feature_rows(totals[5:9])
    count_all = local_rows * n_shard * lax.axis_size("ctx") * D
    root_squares = jnp.sqrt(totals[9] / count_all)

    def whole(parts):
        return jnp.concatenate(ordered(parts, bits), axis=1).astype(F32)

    def whole_halves(parts):
        placed = [ordered(half, bits) for half in parts]
        return jnp.concatenate(
            [placed[half][q] for q in range(4) for half in range(2)], axis=1
        ).astype(F32)

    return (
        result.astype(BF).reshape(1, local_rows, D),
        input_grad.astype(BF).reshape(1, local_rows, D),
        whole(query_grads),
        whole([item[:, :kv_width] for item in kv_grads]),
        whole([item[:, kv_width:] for item in kv_grads]),
        whole(output_grads),
        whole_halves(up_grads),
        whole_halves(down_grads),
        grad_qv_bias,
        grad_up_bias,
        grad_gains,
        grad_biases,
        root_squares,
    )


def solution(mesh):
    if mesh.shape["ctx"] != 4 or mesh.shape["tp"] != 2:
        raise ValueError("unexpected mesh")
    placed = (
        P("shard", "ctx", None),
        P("shard", "ctx", None),
        P("shard", "tp"),
        P("shard", "tp"),
        P("shard", "tp"),
        P("shard", "tp"),
        P("shard", "tp"),
        P("shard", "tp"),
        P(None, "tp", "shard"),
        P("tp", "shard"),
        P(None, "tp", "shard"),
        P(None, "tp", "shard"),
    )
    return jax.shard_map(
        shards,
        mesh=mesh,
        in_specs=placed,
        out_specs=(
            P("shard", "ctx", None),
            P("shard", "ctx", None),
            P("shard", "tp"),
            P("shard", "tp"),
            P("shard", "tp"),
            P("shard", "tp"),
            P("shard", "tp"),
            P("shard", "tp"),
            P(None, "tp", "shard"),
            P("tp", "shard"),
            P(None, "tp", "shard"),
            P(None, "tp", "shard"),
            P(),
        ),
        check_vma=False,
    )
```

```python
import jax
import jax.numpy as jnp
from jax import lax
from jax.experimental import pallas as pl
from jax.experimental.pallas import tpu as pltpu
from jax.sharding import PartitionSpec as P


D = 2048
H = 16
DH = 128
SCALE = DH ** (-0.5)
BF = jnp.bfloat16
F32 = jnp.float32


epsilon = 1e-12


def product(left, right):
    return jnp.dot(left, right, preferred_element_type=F32)


def transposed_times(left, right):
    return lax.dot_general(left, right, (((0,), (0,)), ((), ())), preferred_element_type=F32)


def normalize(stream):
    center = stream - jnp.mean(stream, axis=-1, keepdims=True)
    factor = lax.rsqrt(jnp.mean(center * center, axis=-1, keepdims=True) + epsilon)
    return (center * factor, factor)


def norm_backward(grad_norm, normed, factor):
    return factor * (
        grad_norm
        - jnp.mean(grad_norm, axis=-1, keepdims=True)
        - normed * jnp.mean(grad_norm * normed, axis=-1, keepdims=True)
    )


def gelu_tanh(values):
    return jax.nn.gelu(values, approximate=True)


def contract(left, right, left_axis, right_axis):
    return lax.dot_general(
        left, right, (((left_axis,), (right_axis,)), ((), ())), preferred_element_type=F32
    )


def forward_kernel(q_ref, kh_ref, kn_ref, vh_ref, vn_ref, out_ref, log_ref):
    q = q_ref[...]
    near = contract(kh_ref[...], q, 1, 1) * SCALE
    far = contract(kn_ref[...], q, 1, 1) * SCALE
    peak = jnp.maximum(jnp.max(near, axis=0, keepdims=True), jnp.max(far, axis=0, keepdims=True))
    near = jnp.exp(near - peak)
    far = jnp.exp(far - peak)
    total = jnp.sum(near, axis=0, keepdims=True) + jnp.sum(far, axis=0, keepdims=True)
    out = contract(vh_ref[...], near.astype(BF), 0, 0) + contract(vn_ref[...], far.astype(BF), 0, 0)
    out_ref[...] = (out / total).T.astype(BF)
    log_ref[0] = peak + jnp.log(total)


def backward_kernel(q_ref, kh_ref, kn_ref, vh_ref, vn_ref, grad_ref, log_ref, dq_ref, dkh_ref, dkn_ref, dvh_ref, dvn_ref, *sums):
    step = pl.program_id(1)
    q = q_ref[...]
    grad = grad_ref[...]
    logsum = log_ref[0]
    probs, d_probs = [], []
    for k_ref, v_ref in ((kh_ref, vh_ref), (kn_ref, vn_ref)):
        probs.append(jnp.exp(contract(k_ref[...], q, 1, 1) * SCALE - logsum))
        d_probs.append(contract(v_ref[...], grad, 1, 1))
    inner = sum(jnp.sum(p * d, axis=0, keepdims=True) for p, d in zip(probs, d_probs))
    dq = 0.0
    for at, k_ref in enumerate((kh_ref, kn_ref)):
        d_scores = (probs[at] * (d_probs[at] - inner)).astype(BF)
        dq = dq + contract(k_ref[...], d_scores, 0, 0)
        dk = contract(d_scores, q, 1, 0)
        dv = contract(probs[at].astype(BF), grad, 1, 0)

        @pl.when(step == 0)
        def _():
            sums[at][...] = dk
            sums[2 + at][...] = dv

        @pl.when(step > 0)
        def _():
            sums[at][...] += dk
            sums[2 + at][...] += dv
    dq_ref[...] = (dq * SCALE).T.astype(BF)

    @pl.when(step == pl.num_programs(1) - 1)
    def _():
        dkh_ref[...] = (sums[0][...] * SCALE).astype(BF)
        dkn_ref[...] = (sums[1][...] * SCALE).astype(BF)
        dvh_ref[...] = sums[2][...].astype(BF)
        dvn_ref[...] = sums[3][...].astype(BF)


def kv_specs(rows, heads):
    k = pl.BlockSpec((rows, DH), lambda h, b: (0, h))
    v = pl.BlockSpec((rows, DH), lambda h, b: (0, heads + h))
    return k, k, v, v


def attention(q, kvh, kvn, block=None):
    rows, width = q.shape
    block = block or rows
    heads = width // DH
    row = pl.BlockSpec((block, DH), lambda h, b: (b, h))
    log = pl.BlockSpec((1, 1, block), lambda h, b: (h, 0, b))
    return pl.pallas_call(forward_kernel, grid=(heads, rows // block),
        in_specs=[row, *kv_specs(kvh.shape[0], heads)], out_specs=[row, log],
        out_shape=[jax.ShapeDtypeStruct((rows, width), BF), jax.ShapeDtypeStruct((heads, 1, rows), F32)],
        name="attention_forward")(q, kvh, kvn, kvh, kvn)


def attention_back(q, kvh, kvn, grad, logsum, block=None):
    rows, width = q.shape
    block = block or rows
    heads = width // DH
    keys = kvh.shape[0]
    row = pl.BlockSpec((block, DH), lambda h, b: (b, h))
    log = pl.BlockSpec((1, 1, block), lambda h, b: (h, 0, b))
    k = pl.BlockSpec((keys, DH), lambda h, b: (0, h))
    return pl.pallas_call(backward_kernel, grid=(heads, rows // block),
        in_specs=[row, *kv_specs(keys, heads), row, log],
        out_specs=[row, k, k, k, k],
        out_shape=[jax.ShapeDtypeStruct((rows, width), BF)] + [jax.ShapeDtypeStruct((keys, width), BF)] * 4,
        scratch_shapes=[pltpu.VMEM((keys, DH), F32)] * 4,
        name="attention_backward")(q, kvh, kvn, kvh, kvn, grad, logsum)


def sum_kernel(*refs):
    count = (len(refs) - 1) // 2
    total = 0.0
    for at in range(count):
        total = total + contract(refs[at][...], refs[count + at][...], 1, 1)
    refs[-1][...] = total.astype(refs[-1].dtype)


def sum_products(lefts, rights, block=256):
    rows = lefts[0].shape[0]
    width = rights[0].shape[0]
    return pl.pallas_call(
        sum_kernel,
        grid=(width // block,),
        in_specs=[pl.BlockSpec(left.shape, lambda n: (0, 0)) for left in lefts]
        + [pl.BlockSpec((block, right.shape[1]), lambda n: (n, 0)) for right in rights],
        out_specs=pl.BlockSpec((rows, block), lambda n: (0, n)),
        out_shape=jax.ShapeDtypeStruct((rows, width), BF),
        name="sum_products",
    )(*lefts, *rights)


def after(value, *others):
    return lax.optimization_barrier((value,) + others)[0]


def across(array, step, axis="ctx"):
    size = lax.axis_size(axis)
    return lax.ppermute(array, axis, [(at, at ^ step) for at in range(size)])


def collect(piece):
    return lax.all_gather(piece, "shard", axis=0, tiled=True)


def scatter(total):
    return lax.psum_scatter(total, "shard", scatter_dimension=0, tiled=True)


def scatter_direct(total):
    size = lax.axis_size("shard")
    rows = total.shape[0] // size
    index = lax.axis_index("shard")

    def block(step):
        return lax.dynamic_slice_in_dim(total, ((index + step) % size) * rows, rows, 0)

    got = [
        lax.ppermute(block(step), "shard", [(at, (at + step) % size) for at in range(size)])
        for step in range(1, size)
    ]
    return block(0), got


def sum_direct(mine, got):
    return sum([item.astype(F32) for item in got], mine.astype(F32)).astype(BF)


def fill(own, far):
    return [own, across(own, 1), far, across(far, 1)]


def spread(own):
    return fill(own, across(own, 2))


def near_sums(parts):
    return [
        (parts[q].astype(F32) + across(parts[q + 1], 1).astype(F32)).astype(BF) for q in (0, 2)
    ]


def far_sum(own, far, *hold):
    got = across(far, 2)
    if hold:
        got = after(got, *hold)
    return (own.astype(F32) + got.astype(F32)).astype(BF)


def halves(array):
    width = array.shape[1] // 2
    return [array[:, :width], array[:, width:]]


def join_pair(own, far):
    return fill(far_sum(own, far), far_sum(far, own))


def ordered(pieces, bits):
    low, high = bits
    swapped = [jnp.where(high, pieces[q ^ 2], pieces[q]) for q in range(4)]
    return [jnp.where(low, swapped[q ^ 1], swapped[q]) for q in range(4)]


def tp_sum(low):
    return low.astype(F32) + across(low, 1, "tp").astype(F32)


def butterfly(flat, axes):
    for axis in axes:
        step = 1
        while step < lax.axis_size(axis):
            flat = flat + across(flat, step, axis)
            step *= 2
    return flat


def shards(
    inputs,
    cotangent,
    query_weight,
    key_weight,
    value_weight,
    output_weight,
    up_weight,
    down_weight,
    query_value_bias,
    up_bias,
    norm_gains,
    other_biases,
):
    local_rows = inputs.shape[1]
    member = lax.axis_index("ctx")
    relative = jnp.arange(4) ^ member
    bits = ((member & 1) == 1, (member & 2) == 2)
    n_shard = lax.axis_size("shard")
    n_tp = lax.axis_size("tp")

    def own_columns(weight, step=0):
        width = weight.shape[1] // 4
        return lax.dynamic_slice_in_dim(weight, (member ^ step) * width, width, 1)

    tokens = inputs.reshape(local_rows, D)
    tokens_far = across(tokens, 2)
    grad_out = cotangent.reshape(local_rows, D).astype(F32)

    small = (query_value_bias, norm_gains, other_biases, up_bias)
    packed = jnp.concatenate([item.reshape(1, -1) for item in small], axis=1)
    tp_index = lax.axis_index("tp")
    slot = lax.axis_index("shard") * n_tp + tp_index
    packed_all = lax.dynamic_update_slice_in_dim(
        jnp.zeros((n_shard * n_tp, packed.shape[1]), BF), packed, slot, 0
    )
    packed_all = butterfly(packed_all, ("tp", "shard"))
    packed_all = packed_all.reshape(n_shard, n_tp, packed.shape[1])
    at = 0
    small_all = []
    for item in small:
        part = packed_all[:, :, at : at + item.size].reshape((n_shard, n_tp) + item.shape)
        at += item.size
        small_all.append(part)
    qv_all = lax.dynamic_index_in_dim(small_all[0], tp_index, 1, False)
    qv_half = qv_all.transpose(1, 2, 0, 3).reshape(2, 4, -1).astype(F32)
    qv_vector = jnp.take(qv_half, relative, axis=1)
    gains = small_all[1].transpose(2, 1, 3, 0, 4).reshape(2, D).astype(F32)
    biases = small_all[2].transpose(2, 1, 3, 0, 4).reshape(4, D).astype(F32)
    up_all = lax.dynamic_index_in_dim(small_all[3], tp_index, 1, False)
    up_vector = jnp.take(up_all.transpose(1, 0, 2).reshape(4, -1).astype(F32), relative, axis=0)

    kv_width = key_weight.shape[1] // 4
    heads_each = kv_width // DH
    heads_here = 4 * heads_each
    ff_half = up_weight.shape[1] // 8
    kv_own = collect(jnp.concatenate([own_columns(key_weight), own_columns(value_weight)], axis=1))
    pair_own = collect(
        jnp.concatenate([own_columns(query_weight), own_columns(output_weight)], axis=1)
    )
    up_piece = own_columns(up_weight)
    down_piece = own_columns(down_weight)
    up_own = [collect(up_piece[:, half * ff_half : (half + 1) * ff_half]) for half in range(2)]
    down_own = [collect(down_piece[:, half * ff_half : (half + 1) * ff_half]) for half in range(2)]
    ff_part = ff_half // 2
    down_far = collect(own_columns(down_weight, 2)[:, ff_half + ff_part :])
    key_value_w = fill(kv_own, across(after(kv_own, tokens_far), 2))
    pair_far = after(across(pair_own, 2), kv_own)
    pair_w = fill(pair_own, pair_far)
    query_w = [item[:, :kv_width] for item in pair_w]
    output_w = [item[:, kv_width:] for item in pair_w]

    tokens_two = jnp.concatenate([tokens, tokens_far], axis=0)
    zero_row = jnp.zeros((kv_width,), F32)
    kv_here = [
        (
            product(tokens_two, key_value_w[q]) + jnp.concatenate([zero_row, qv_vector[1, q]])
        ).astype(BF)
        for q in range(4)
    ]
    kv_near = [across(kv_here[q ^ 1], 1) for q in range(4)]
    queries = [(product(tokens, query_w[q]) + qv_vector[0, q]).astype(BF) for q in range(4)]
    attended, logsums = [], []
    for q in range(4):
        out, log = attention(queries[q], kv_here[q], kv_near[q])
        attended.append(out)
        logsums.append(log)
    attn_low = sum_products(attended, output_w)
    up_far = across(up_own[0], 2)
    up_w = [fill(up_own[0], up_far), spread(after(up_own[1], attended[3]))]
    attn_branch = tp_sum(attn_low) + biases[0]
    normed_one, factor_one = normalize(tokens.astype(F32) + attn_branch)
    hidden_one = normed_one * gains[0] + biases[1]
    hidden_low = hidden_one.astype(BF)

    pairs = [(half, q) for half in range(2) for q in range(4)]
    up_rows = up_vector.reshape(4, 2, ff_half)
    pre_act = [product(hidden_low, up_w[half][q]) + up_rows[q, half] for half, q in pairs]
    activated = [gelu_tanh(item).astype(BF) for item in pre_act]
    down_swapped = across(after(down_own[1], *activated)[:, :ff_part], 2)
    down_last = jnp.concatenate([down_swapped, after(down_far, *activated)], axis=1)
    down_w = [
        spread(after(down_own[0], activated[0])),
        fill(down_own[1], down_last),
    ]
    mlp_low = sum_products(activated, [down_w[half][q] for half, q in pairs])
    mlp_branch = tp_sum(mlp_low) + biases[2]
    second = hidden_one + mlp_branch
    normed_two, factor_two = normalize(second)
    result = normed_two * gains[1] + biases[3]
    grad_second = norm_backward(grad_out * gains[1], normed_two, factor_two)
    grad_mlp = grad_second.astype(BF)
    down_parts = [transposed_times(grad_mlp, item).astype(BF) for item in activated]
    down_late = near_sums(down_parts[4:8])
    down_early = near_sums(down_parts[0:4])
    down_late = jnp.concatenate(down_late, axis=1)
    grad_mlp_then = after(grad_mlp, down_late, *down_early)
    down_second = scatter(down_late)
    grad_pre = []
    for at, (half, q) in enumerate(pairs):
        _, gelu_pull = jax.vjp(gelu_tanh, pre_act[at])
        grad_pre.append(gelu_pull(product(grad_mlp_then, down_w[half][q]))[0].astype(BF))
    hidden_part = sum_products(grad_pre, [up_w[half][q] for half, q in pairs])
    down_total = far_sum(*down_early, hidden_part)
    down_first = scatter(down_total)
    up_parts = [transposed_times(hidden_low, item).astype(BF) for item in grad_pre]
    up_early = near_sums(up_parts[0:4])
    up_late = jnp.concatenate(near_sums(up_parts[4:8]), axis=1)
    up_second = scatter(up_late)
    hidden_got = after(across(hidden_part, 1, "tp"), down_total, up_late, *up_early)
    grad_hidden = grad_second + (hidden_part.astype(F32) + hidden_got.astype(F32))
    down_second = halves(down_second)
    down_pair = [far_sum(*down_second), far_sum(*down_second[::-1])]
    grad_first = norm_backward(grad_hidden * gains[0], normed_one, factor_one)
    grad_branch = grad_first.astype(BF)
    grad_attended = [product(grad_branch, output_w[q]).astype(BF) for q in range(4)]
    up_total = far_sum(*up_early, grad_branch)
    up_first = scatter(up_total)
    output_early = near_sums(
        [transposed_times(grad_branch, attended[q]).astype(BF) for q in range(4)]
    )
    grad_attended[2:] = lax.optimization_barrier((*grad_attended[2:], up_total))[:-1]
    down_far_first = across(down_first, 2)
    grad_q, here_parts, near_parts = [], [], []
    for q in range(4):
        dq, dk_here, dk_near, dv_here, dv_near = attention_back(
            queries[q], kv_here[q], kv_near[q], grad_attended[q], logsums[q]
        )
        grad_q.append(dq)
        here_parts.append((dk_here, dv_here))
        near_parts.append((across(dk_near, 1), across(dv_near, 1)))
    two_sums = [
        jnp.concatenate(
            [
                (here_parts[q][at].astype(F32) + near_parts[q ^ 1][at].astype(F32)).astype(BF)
                for at in range(2)
            ],
            axis=1,
        )
        for q in range(4)
    ]
    far_sums = [across(two_sums[q][local_rows:], 2) for q in range(4)]
    grad_kv = [
        (two_sums[q][:local_rows].astype(F32) + far_sums[q ^ 2].astype(F32)).astype(BF)
        for q in range(4)
    ]
    output_direct = scatter_direct(far_sum(*output_early, *grad_q))
    query_early = near_sums([transposed_times(tokens, grad_q[q]).astype(BF) for q in range(4)])
    kv_parts = [transposed_times(tokens, grad_kv[q]).astype(BF) for q in range(4)]
    kv_total = far_sum(*near_sums(kv_parts))
    kv_mine = scatter(kv_total)
    query_mine, query_got = scatter_direct(far_sum(*query_early, kv_total))
    output_mine, output_got = lax.optimization_barrier((*output_direct, kv_total))[:2]
    up_first, up_second, grad_q_then = (
        after(item, kv_total) for item in (up_first, up_second, grad_q[0])
    )
    down_grads = [fill(down_first, down_far_first), fill(*down_pair)]
    up_grads = [spread(up_first), join_pair(*halves(up_second))]
    output_grads = spread(sum_direct(output_mine, output_got))
    query_grads = spread(sum_direct(query_mine, query_got))
    kv_grads = spread(kv_mine)
    input_part = sum_products([grad_q_then] + grad_q[1:] + grad_kv, query_w + key_value_w)
    input_grad = grad_first + tp_sum(input_part)

    def canonical(rows):
        return jnp.take(jnp.stack(rows), relative, axis=0).reshape(-1)

    def column_sums(array):
        return jnp.sum(array.astype(F32), axis=0)

    pieces = [
        canonical([column_sums(grad_q[q]) for q in range(4)]),
        canonical([column_sums(grad_kv[q][:, kv_width:]) for q in range(4)]),
        canonical(
            [
                jnp.concatenate([column_sums(grad_pre[q]), column_sums(grad_pre[4 + q])])
                for q in range(4)
            ]
        ),
        jnp.sum(grad_hidden * normed_one, axis=0),
        jnp.sum(grad_out * normed_two, axis=0),
        column_sums(grad_branch),
        jnp.sum(grad_hidden, axis=0),
        column_sums(grad_mlp),
        jnp.sum(grad_out, axis=0),
        jnp.stack(
            [
                jnp.sum(second * second),
                jnp.sum(attn_branch * attn_branch),
                jnp.sum(mlp_branch * mlp_branch),
            ]
        ),
    ]
    sizes = [item.shape[0] for item in pieces]
    flat = jnp.concatenate(pieces + [jnp.zeros((-sum(sizes) % 1024,), F32)]).reshape(-1, 128)
    flat = butterfly(after(flat, kv_total), ("ctx", "shard")).reshape(-1)
    totals = []
    at = 0
    for size in sizes:
        totals.append(flat[at : at + size])
        at += size
    shard_index = lax.axis_index("shard")
    piece = DH // n_shard
    heads_part = H // n_tp

    def last_piece(array, axis):
        return lax.dynamic_slice_in_dim(array, shard_index * piece, piece, axis)

    grad_qv_bias = last_piece(jnp.stack(totals[0:2]).reshape(2, heads_here, DH), 2)
    grad_up_bias = last_piece(totals[2].reshape(-1, DH), 1)

    def feature_rows(rows):
        stacked = jnp.stack(rows).reshape(len(rows), H, DH)
        return last_piece(
            lax.dynamic_slice_in_dim(stacked, tp_index * heads_part, heads_part, 1), 2
        )

    grad_gains = feature_rows(totals[3:5])
    grad_biases = feature_rows(totals[5:9])
    count_all = local_rows * n_shard * lax.axis_size("ctx") * D
    root_squares = jnp.sqrt(totals[9] / count_all)

    def whole(parts):
        return jnp.concatenate(ordered(parts, bits), axis=1).astype(F32)

    def whole_halves(parts):
        placed = [ordered(half, bits) for half in parts]
        return jnp.concatenate(
            [placed[half][q] for q in range(4) for half in range(2)], axis=1
        ).astype(F32)

    return (
        result.astype(BF).reshape(1, local_rows, D),
        input_grad.astype(BF).reshape(1, local_rows, D),
        whole(query_grads),
        whole([item[:, :kv_width] for item in kv_grads]),
        whole([item[:, kv_width:] for item in kv_grads]),
        whole(output_grads),
        whole_halves(up_grads),
        whole_halves(down_grads),
        grad_qv_bias,
        grad_up_bias,
        grad_gains,
        grad_biases,
        root_squares,
    )


def solution(mesh):
    if mesh.shape["ctx"] != 4 or mesh.shape["tp"] != 2:
        raise ValueError("unexpected mesh")
    placed = (
        P("shard", "ctx", None),
        P("shard", "ctx", None),
        P("shard", "tp"),
        P("shard", "tp"),
        P("shard", "tp"),
        P("shard", "tp"),
        P("shard", "tp"),
        P("shard", "tp"),
        P(None, "tp", "shard"),
        P("tp", "shard"),
        P(None, "tp", "shard"),
        P(None, "tp", "shard"),
    )
    return jax.shard_map(
        shards,
        mesh=mesh,
        in_specs=placed,
        out_specs=(
            P("shard", "ctx", None),
            P("shard", "ctx", None),
            P("shard", "tp"),
            P("shard", "tp"),
            P("shard", "tp"),
            P("shard", "tp"),
            P("shard", "tp"),
            P("shard", "tp"),
            P(None, "tp", "shard"),
            P("tp", "shard"),
            P(None, "tp", "shard"),
            P(None, "tp", "shard"),
            P(),
        ),
        check_vma=False,
    )
```

```python
import jax
import jax.numpy as jnp
from jax import lax
from jax.experimental import pallas as pl
from jax.experimental.pallas import tpu as pltpu
from jax.experimental.layout import Layout, with_layout_constraint
from jax.sharding import PartitionSpec as P


D = 2048
H = 16
DH = 128
SCALE = DH ** (-0.5)
BF = jnp.bfloat16
F32 = jnp.float32


epsilon = 1e-12


def product(left, right):
    return jnp.dot(left, right, preferred_element_type=F32)


def transposed_times(left, right):
    return lax.dot_general(left, right, (((0,), (0,)), ((), ())), preferred_element_type=F32)


def normalize(stream):
    center = stream - jnp.mean(stream, axis=-1, keepdims=True)
    factor = lax.rsqrt(jnp.mean(center * center, axis=-1, keepdims=True) + epsilon)
    return (center * factor, factor)


def norm_backward(grad_norm, normed, factor):
    return factor * (
        grad_norm
        - jnp.mean(grad_norm, axis=-1, keepdims=True)
        - normed * jnp.mean(grad_norm * normed, axis=-1, keepdims=True)
    )


def gelu_tanh(values):
    return jax.nn.gelu(values, approximate=True)


def contract(left, right, left_axis, right_axis):
    return lax.dot_general(
        left, right, (((left_axis,), (right_axis,)), ((), ())), preferred_element_type=F32
    )


def forward_kernel(q_ref, kh_ref, kn_ref, vh_ref, vn_ref, out_ref, log_ref):
    q = q_ref[...]
    near = contract(kh_ref[...], q, 1, 1) * SCALE
    far = contract(kn_ref[...], q, 1, 1) * SCALE
    peak = jnp.maximum(jnp.max(near, axis=0, keepdims=True), jnp.max(far, axis=0, keepdims=True))
    near = jnp.exp(near - peak)
    far = jnp.exp(far - peak)
    total = jnp.sum(near, axis=0, keepdims=True) + jnp.sum(far, axis=0, keepdims=True)
    out = contract(vh_ref[...], near.astype(BF), 0, 0) + contract(vn_ref[...], far.astype(BF), 0, 0)
    out_ref[...] = (out / total).T.astype(BF)
    log_ref[0] = peak + jnp.log(total)


def backward_kernel(q_ref, kh_ref, kn_ref, vh_ref, vn_ref, grad_ref, log_ref, dq_ref, dkh_ref, dkn_ref, dvh_ref, dvn_ref, *sums):
    step = pl.program_id(1)
    q = q_ref[...]
    grad = grad_ref[...]
    logsum = log_ref[0]
    probs, d_probs = [], []
    for k_ref, v_ref in ((kh_ref, vh_ref), (kn_ref, vn_ref)):
        probs.append(jnp.exp(contract(k_ref[...], q, 1, 1) * SCALE - logsum))
        d_probs.append(contract(v_ref[...], grad, 1, 1))
    inner = sum(jnp.sum(p * d, axis=0, keepdims=True) for p, d in zip(probs, d_probs))
    dq = 0.0
    for at, k_ref in enumerate((kh_ref, kn_ref)):
        d_scores = (probs[at] * (d_probs[at] - inner)).astype(BF)
        dq = dq + contract(k_ref[...], d_scores, 0, 0)
        dk = contract(d_scores, q, 1, 0)
        dv = contract(probs[at].astype(BF), grad, 1, 0)

        @pl.when(step == 0)
        def _():
            sums[at][...] = dk
            sums[2 + at][...] = dv

        @pl.when(step > 0)
        def _():
            sums[at][...] += dk
            sums[2 + at][...] += dv
    dq_ref[...] = (dq * SCALE).T.astype(BF)

    @pl.when(step == pl.num_programs(1) - 1)
    def _():
        dkh_ref[...] = (sums[0][...] * SCALE).astype(BF)
        dkn_ref[...] = (sums[1][...] * SCALE).astype(BF)
        dvh_ref[...] = sums[2][...].astype(BF)
        dvn_ref[...] = sums[3][...].astype(BF)


def kv_specs(rows, heads):
    k = pl.BlockSpec((rows, DH), lambda h, b: (0, h))
    v = pl.BlockSpec((rows, DH), lambda h, b: (0, heads + h))
    return k, k, v, v


def attention(q, kvh, kvn, block=None):
    rows, width = q.shape
    block = block or rows
    heads = width // DH
    row = pl.BlockSpec((block, DH), lambda h, b: (b, h))
    log = pl.BlockSpec((1, 1, block), lambda h, b: (h, 0, b))
    return pl.pallas_call(forward_kernel, grid=(heads, rows // block),
        in_specs=[row, *kv_specs(kvh.shape[0], heads)], out_specs=[row, log],
        out_shape=[jax.ShapeDtypeStruct((rows, width), BF), jax.ShapeDtypeStruct((heads, 1, rows), F32)],
        name="attention_forward")(q, kvh, kvn, kvh, kvn)


def attention_back(q, kvh, kvn, grad, logsum, block=None):
    rows, width = q.shape
    block = block or rows
    heads = width // DH
    keys = kvh.shape[0]
    row = pl.BlockSpec((block, DH), lambda h, b: (b, h))
    log = pl.BlockSpec((1, 1, block), lambda h, b: (h, 0, b))
    k = pl.BlockSpec((keys, DH), lambda h, b: (0, h))
    return pl.pallas_call(backward_kernel, grid=(heads, rows // block),
        in_specs=[row, *kv_specs(keys, heads), row, log],
        out_specs=[row, k, k, k, k],
        out_shape=[jax.ShapeDtypeStruct((rows, width), BF)] + [jax.ShapeDtypeStruct((keys, width), BF)] * 4,
        scratch_shapes=[pltpu.VMEM((keys, DH), F32)] * 4,
        name="attention_backward")(q, kvh, kvn, kvh, kvn, grad, logsum)


def sum_kernel(*refs):
    count = (len(refs) - 1) // 2
    total = 0.0
    for at in range(count):
        total = total + contract(refs[at][...], refs[count + at][...], 1, 1)
    refs[-1][...] = total.astype(refs[-1].dtype)


def sum_products(lefts, rights, block=256):
    rows = lefts[0].shape[0]
    width = rights[0].shape[0]
    return pl.pallas_call(
        sum_kernel,
        grid=(width // block,),
        in_specs=[pl.BlockSpec(left.shape, lambda n: (0, 0)) for left in lefts]
        + [pl.BlockSpec((block, right.shape[1]), lambda n: (n, 0)) for right in rights],
        out_specs=pl.BlockSpec((rows, block), lambda n: (0, n)),
        out_shape=jax.ShapeDtypeStruct((rows, width), BF),
        name="sum_products",
    )(*lefts, *rights)


def after(value, *others):
    return lax.optimization_barrier((value,) + others)[0]


def across(array, step, axis="ctx"):
    size = lax.axis_size(axis)
    return lax.ppermute(array, axis, [(at, at ^ step) for at in range(size)])


def collect(piece):
    return lax.all_gather(piece, "shard", axis=0, tiled=True)


def scatter(total):
    mine = lax.psum_scatter(total, "shard", scatter_dimension=0, tiled=True)
    return with_layout_constraint(mine, Layout((0, 1)))


def scatter_direct(total):
    size = lax.axis_size("shard")
    rows = total.shape[0] // size
    index = lax.axis_index("shard")

    def block(step):
        return lax.dynamic_slice_in_dim(total, ((index + step) % size) * rows, rows, 0)

    got = [
        lax.ppermute(block(step), "shard", [(at, (at + step) % size) for at in range(size)])
        for step in range(1, size)
    ]
    return block(0), got


def sum_direct(mine, got):
    total = sum([item.astype(F32) for item in got], mine.astype(F32)).astype(BF)
    return with_layout_constraint(total, Layout((0, 1)))


def fill(own, far):
    return [own, across(own, 1), far, across(far, 1)]


def spread(own):
    return fill(own, across(own, 2))


def near_sums(parts):
    return [
        (parts[q].astype(F32) + across(parts[q + 1], 1).astype(F32)).astype(BF) for q in (0, 2)
    ]


def far_sum(own, far, *hold):
    got = across(far, 2)
    if hold:
        got = after(got, *hold)
    return (own.astype(F32) + got.astype(F32)).astype(BF)


def halves(array):
    width = array.shape[1] // 2
    return [array[:, :width], array[:, width:]]


def join_pair(own, far):
    return fill(far_sum(own, far), far_sum(far, own))


def ordered(pieces, bits):
    low, high = bits
    swapped = [jnp.where(high, pieces[q ^ 2], pieces[q]) for q in range(4)]
    return [jnp.where(low, swapped[q ^ 1], swapped[q]) for q in range(4)]


def tp_sum(low):
    return low.astype(F32) + across(low, 1, "tp").astype(F32)


def butterfly(flat, axes):
    for axis in axes:
        step = 1
        while step < lax.axis_size(axis):
            flat = flat + across(flat, step, axis)
            step *= 2
    return flat


def shards(
    inputs,
    cotangent,
    query_weight,
    key_weight,
    value_weight,
    output_weight,
    up_weight,
    down_weight,
    query_value_bias,
    up_bias,
    norm_gains,
    other_biases,
):
    local_rows = inputs.shape[1]
    member = lax.axis_index("ctx")
    relative = jnp.arange(4) ^ member
    bits = ((member & 1) == 1, (member & 2) == 2)
    n_shard = lax.axis_size("shard")
    n_tp = lax.axis_size("tp")

    def own_columns(weight, step=0):
        width = weight.shape[1] // 4
        return lax.dynamic_slice_in_dim(weight, (member ^ step) * width, width, 1)

    tokens = inputs.reshape(local_rows, D)
    tokens_far = across(tokens, 2)
    grad_out = cotangent.reshape(local_rows, D).astype(F32)

    small = (query_value_bias, norm_gains, other_biases, up_bias)
    packed = jnp.concatenate([item.reshape(1, -1) for item in small], axis=1)
    tp_index = lax.axis_index("tp")
    slot = lax.axis_index("shard") * n_tp + tp_index
    packed_all = lax.dynamic_update_slice_in_dim(
        jnp.zeros((n_shard * n_tp, packed.shape[1]), BF), packed, slot, 0
    )
    packed_all = butterfly(packed_all, ("tp", "shard"))
    packed_all = packed_all.reshape(n_shard, n_tp, packed.shape[1])
    at = 0
    small_all = []
    for item in small:
        part = packed_all[:, :, at : at + item.size].reshape((n_shard, n_tp) + item.shape)
        at += item.size
        small_all.append(part)
    qv_all = lax.dynamic_index_in_dim(small_all[0], tp_index, 1, False)
    qv_half = qv_all.transpose(1, 2, 0, 3).reshape(2, 4, -1).astype(F32)
    qv_vector = jnp.take(qv_half, relative, axis=1)
    gains = small_all[1].transpose(2, 1, 3, 0, 4).reshape(2, D).astype(F32)
    biases = small_all[2].transpose(2, 1, 3, 0, 4).reshape(4, D).astype(F32)
    up_all = lax.dynamic_index_in_dim(small_all[3], tp_index, 1, False)
    up_vector = jnp.take(up_all.transpose(1, 0, 2).reshape(4, -1).astype(F32), relative, axis=0)

    kv_width = key_weight.shape[1] // 4
    heads_each = kv_width // DH
    heads_here = 4 * heads_each
    ff_half = up_weight.shape[1] // 8
    kv_own = collect(jnp.concatenate([own_columns(key_weight), own_columns(value_weight)], axis=1))
    pair_own = collect(
        jnp.concatenate([own_columns(query_weight), own_columns(output_weight)], axis=1)
    )
    up_piece = own_columns(up_weight)
    down_piece = own_columns(down_weight)
    up_own = [collect(up_piece[:, half * ff_half : (half + 1) * ff_half]) for half in range(2)]
    down_own = [collect(down_piece[:, half * ff_half : (half + 1) * ff_half]) for half in range(2)]
    ff_part = ff_half // 2
    down_far = collect(own_columns(down_weight, 2)[:, ff_half + ff_part :])
    key_value_w = fill(kv_own, across(after(kv_own, tokens_far), 2))
    pair_far = after(across(pair_own, 2), kv_own)
    pair_w = fill(pair_own, pair_far)
    query_w = [item[:, :kv_width] for item in pair_w]
    output_w = [item[:, kv_width:] for item in pair_w]

    tokens_two = jnp.concatenate([tokens, tokens_far], axis=0)
    zero_row = jnp.zeros((kv_width,), F32)
    kv_here = [
        (
            product(tokens_two, key_value_w[q]) + jnp.concatenate([zero_row, qv_vector[1, q]])
        ).astype(BF)
        for q in range(4)
    ]
    kv_near = [across(kv_here[q ^ 1], 1) for q in range(4)]
    queries = [(product(tokens, query_w[q]) + qv_vector[0, q]).astype(BF) for q in range(4)]
    attended, logsums = [], []
    for q in range(4):
        out, log = attention(queries[q], kv_here[q], kv_near[q])
        attended.append(out)
        logsums.append(log)
    attn_low = sum_products(attended, output_w)
    up_far = across(up_own[0], 2)
    up_w = [fill(up_own[0], up_far), spread(after(up_own[1], attended[3]))]
    attn_branch = tp_sum(attn_low) + biases[0]
    normed_one, factor_one = normalize(tokens.astype(F32) + attn_branch)
    hidden_one = normed_one * gains[0] + biases[1]
    hidden_low = hidden_one.astype(BF)

    pairs = [(half, q) for half in range(2) for q in range(4)]
    up_rows = up_vector.reshape(4, 2, ff_half)
    pre_act = [product(hidden_low, up_w[half][q]) + up_rows[q, half] for half, q in pairs]
    activated = [gelu_tanh(item).astype(BF) for item in pre_act]
    down_swapped = across(after(down_own[1], activated[0])[:, :ff_part], 2)
    down_last = jnp.concatenate([down_swapped, after(down_far, *activated)], axis=1)
    down_w = [
        spread(after(down_own[0], activated[0])),
        fill(down_own[1], down_last),
    ]
    mlp_low = sum_products(activated, [down_w[half][q] for half, q in pairs])
    mlp_branch = tp_sum(mlp_low) + biases[2]
    second = hidden_one + mlp_branch
    normed_two, factor_two = normalize(second)
    result = normed_two * gains[1] + biases[3]
    grad_second = norm_backward(grad_out * gains[1], normed_two, factor_two)
    grad_mlp = grad_second.astype(BF)
    down_parts = [transposed_times(grad_mlp, item).astype(BF) for item in activated]
    down_late = near_sums(down_parts[4:8])
    down_early = near_sums(down_parts[0:4])
    down_late = jnp.concatenate(down_late, axis=1)
    grad_mlp_then = after(grad_mlp, down_late, *down_early)
    down_second = scatter(down_late)
    grad_pre = []
    for at, (half, q) in enumerate(pairs):
        _, gelu_pull = jax.vjp(gelu_tanh, pre_act[at])
        grad_pre.append(gelu_pull(product(grad_mlp_then, down_w[half][q]))[0].astype(BF))
    hidden_part = sum_products(grad_pre, [up_w[half][q] for half, q in pairs])
    down_total = far_sum(*down_early, hidden_part)
    down_first = scatter(down_total)
    up_parts = [transposed_times(hidden_low, item).astype(BF) for item in grad_pre]
    up_early = near_sums(up_parts[0:4])
    up_late = jnp.concatenate(near_sums(up_parts[4:8]), axis=1)
    up_second = scatter(up_late)
    hidden_got = after(across(hidden_part, 1, "tp"), down_total, up_late, *up_early)
    grad_hidden = grad_second + (hidden_part.astype(F32) + hidden_got.astype(F32))
    down_second = halves(down_second)
    down_pair = [far_sum(*down_second), far_sum(*down_second[::-1])]
    grad_first = norm_backward(grad_hidden * gains[0], normed_one, factor_one)
    grad_branch = grad_first.astype(BF)
    grad_attended = [product(grad_branch, output_w[q]).astype(BF) for q in range(4)]
    up_total = far_sum(*up_early, grad_branch)
    up_first = scatter(up_total)
    output_early = near_sums(
        [transposed_times(grad_branch, attended[q]).astype(BF) for q in range(4)]
    )
    grad_attended[1:] = lax.optimization_barrier((*grad_attended[1:], *output_early))[:3]
    grad_attended[2:] = lax.optimization_barrier((*grad_attended[2:], up_total))[:-1]
    down_far_first = across(down_first, 2)
    grad_q, here_parts, near_parts = [], [], []
    for q in range(4):
        dq, dk_here, dk_near, dv_here, dv_near = attention_back(
            queries[q], kv_here[q], kv_near[q], grad_attended[q], logsums[q]
        )
        grad_q.append(dq)
        here_parts.append((dk_here, dv_here))
        near_parts.append((across(dk_near, 1), across(dv_near, 1)))
    two_sums = [
        jnp.concatenate(
            [
                (here_parts[q][at].astype(F32) + near_parts[q ^ 1][at].astype(F32)).astype(BF)
                for at in range(2)
            ],
            axis=1,
        )
        for q in range(4)
    ]
    far_sums = [across(two_sums[q][local_rows:], 2) for q in range(4)]
    grad_kv = [
        (two_sums[q][:local_rows].astype(F32) + far_sums[q ^ 2].astype(F32)).astype(BF)
        for q in range(4)
    ]
    output_direct = scatter_direct(far_sum(*output_early, *grad_q))
    query_early = near_sums([transposed_times(tokens, grad_q[q]).astype(BF) for q in range(4)])
    kv_parts = [transposed_times(tokens, grad_kv[q]).astype(BF) for q in range(4)]
    kv_early = near_sums(kv_parts)
    kv_total = far_sum(*kv_early)
    kv_mine = scatter(kv_total)
    query_mine, query_got = scatter_direct(
        far_sum(query_early[0], after(query_early[1], kv_total))
    )
    output_mine, output_got = lax.optimization_barrier((*output_direct, kv_total))[:2]
    up_first, up_second, grad_q_then = (
        after(item, kv_total) for item in (up_first, up_second, grad_q[0])
    )
    down_grads = [fill(down_first, down_far_first), fill(*down_pair)]
    up_grads = [spread(up_first), join_pair(*halves(up_second))]
    output_grads = spread(sum_direct(output_mine, output_got))
    query_grads = spread(sum_direct(query_mine, query_got))
    kv_grads = spread(kv_mine)
    input_part = sum_products([grad_q_then] + grad_q[1:] + grad_kv, query_w + key_value_w)
    input_grad = grad_first + tp_sum(input_part)

    def canonical(rows):
        return jnp.take(jnp.stack(rows), relative, axis=0).reshape(-1)

    def column_sums(array):
        return jnp.sum(array.astype(F32), axis=0)

    pieces = [
        canonical([column_sums(grad_q[q]) for q in range(4)]),
        canonical([column_sums(grad_kv[q][:, kv_width:]) for q in range(4)]),
        canonical(
            [
                jnp.concatenate([column_sums(grad_pre[q]), column_sums(grad_pre[4 + q])])
                for q in range(4)
            ]
        ),
        jnp.sum(grad_hidden * normed_one, axis=0),
        jnp.sum(grad_out * normed_two, axis=0),
        column_sums(grad_branch),
        jnp.sum(grad_hidden, axis=0),
        column_sums(grad_mlp),
        jnp.sum(grad_out, axis=0),
        jnp.stack(
            [
                jnp.sum(second * second),
                jnp.sum(attn_branch * attn_branch),
                jnp.sum(mlp_branch * mlp_branch),
            ]
        ),
    ]
    sizes = [item.shape[0] for item in pieces]
    flat = jnp.concatenate(pieces + [jnp.zeros((-sum(sizes) % 1024,), F32)]).reshape(-1, 128)
    flat = butterfly(after(flat, *kv_early), ("ctx", "shard")).reshape(-1)
    totals = []
    at = 0
    for size in sizes:
        totals.append(flat[at : at + size])
        at += size
    shard_index = lax.axis_index("shard")
    piece = DH // n_shard
    heads_part = H // n_tp

    def last_piece(array, axis):
        return lax.dynamic_slice_in_dim(array, shard_index * piece, piece, axis)

    grad_qv_bias = last_piece(jnp.stack(totals[0:2]).reshape(2, heads_here, DH), 2)
    grad_up_bias = last_piece(totals[2].reshape(-1, DH), 1)

    def feature_rows(rows):
        stacked = jnp.stack(rows).reshape(len(rows), H, DH)
        return last_piece(
            lax.dynamic_slice_in_dim(stacked, tp_index * heads_part, heads_part, 1), 2
        )

    grad_gains = feature_rows(totals[3:5])
    grad_biases = feature_rows(totals[5:9])
    count_all = local_rows * n_shard * lax.axis_size("ctx") * D
    root_squares = jnp.sqrt(totals[9] / count_all)

    def whole(parts):
        return jnp.concatenate(ordered(parts, bits), axis=1).astype(F32)

    def whole_halves(parts):
        placed = [ordered(half, bits) for half in parts]
        return jnp.concatenate(
            [placed[half][q] for q in range(4) for half in range(2)], axis=1
        ).astype(F32)

    return (
        result.astype(BF).reshape(1, local_rows, D),
        input_grad.astype(BF).reshape(1, local_rows, D),
        whole(query_grads),
        whole([item[:, :kv_width] for item in kv_grads]),
        whole([item[:, kv_width:] for item in kv_grads]),
        whole(output_grads),
        whole_halves(up_grads),
        whole_halves(down_grads),
        grad_qv_bias,
        grad_up_bias,
        grad_gains,
        grad_biases,
        root_squares,
    )


def solution(mesh):
    if mesh.shape["ctx"] != 4 or mesh.shape["tp"] != 2:
        raise ValueError("unexpected mesh")
    placed = (
        P("shard", "ctx", None),
        P("shard", "ctx", None),
        P("shard", "tp"),
        P("shard", "tp"),
        P("shard", "tp"),
        P("shard", "tp"),
        P("shard", "tp"),
        P("shard", "tp"),
        P(None, "tp", "shard"),
        P("tp", "shard"),
        P(None, "tp", "shard"),
        P(None, "tp", "shard"),
    )
    return jax.shard_map(
        shards,
        mesh=mesh,
        in_specs=placed,
        out_specs=(
            P("shard", "ctx", None),
            P("shard", "ctx", None),
            P("shard", "tp"),
            P("shard", "tp"),
            P("shard", "tp"),
            P("shard", "tp"),
            P("shard", "tp"),
            P("shard", "tp"),
            P(None, "tp", "shard"),
            P("tp", "shard"),
            P(None, "tp", "shard"),
            P(None, "tp", "shard"),
            P(),
        ),
        check_vma=False,
    )
```

```python
import jax
import jax.numpy as jnp
from jax import lax
from jax.experimental import pallas as pl
from jax.experimental.pallas import tpu as pltpu
from jax.experimental.layout import Layout, with_layout_constraint
from jax.sharding import PartitionSpec as P


D = 2048
H = 16
DH = 128
SCALE = DH ** (-0.5)
BF = jnp.bfloat16
F32 = jnp.float32


epsilon = 1e-12


def product(left, right):
    return jnp.dot(left, right, preferred_element_type=F32)


def transposed_times(left, right):
    return lax.dot_general(left, right, (((0,), (0,)), ((), ())), preferred_element_type=F32)


def normalize(stream):
    center = stream - jnp.mean(stream, axis=-1, keepdims=True)
    factor = lax.rsqrt(jnp.mean(center * center, axis=-1, keepdims=True) + epsilon)
    return (center * factor, factor)


def norm_backward(grad_norm, normed, factor):
    return factor * (
        grad_norm
        - jnp.mean(grad_norm, axis=-1, keepdims=True)
        - normed * jnp.mean(grad_norm * normed, axis=-1, keepdims=True)
    )


def gelu_tanh(values):
    return jax.nn.gelu(values, approximate=True)


def contract(left, right, left_axis, right_axis):
    return lax.dot_general(
        left, right, (((left_axis,), (right_axis,)), ((), ())), preferred_element_type=F32
    )


def forward_kernel(q_ref, kh_ref, kn_ref, vh_ref, vn_ref, out_ref, log_ref):
    q = q_ref[...]
    near = contract(kh_ref[...], q, 1, 1) * SCALE
    far = contract(kn_ref[...], q, 1, 1) * SCALE
    peak = jnp.maximum(jnp.max(near, axis=0, keepdims=True), jnp.max(far, axis=0, keepdims=True))
    near = jnp.exp(near - peak)
    far = jnp.exp(far - peak)
    total = jnp.sum(near, axis=0, keepdims=True) + jnp.sum(far, axis=0, keepdims=True)
    out = contract(vh_ref[...], near.astype(BF), 0, 0) + contract(vn_ref[...], far.astype(BF), 0, 0)
    out_ref[...] = (out / total).T.astype(BF)
    log_ref[0] = peak + jnp.log(total)


def backward_kernel(q_ref, kh_ref, kn_ref, vh_ref, vn_ref, grad_ref, log_ref, dq_ref, dkh_ref, dkn_ref, dvh_ref, dvn_ref, *sums):
    step = pl.program_id(1)
    q = q_ref[...]
    grad = grad_ref[...]
    logsum = log_ref[0]
    probs, d_probs = [], []
    for k_ref, v_ref in ((kh_ref, vh_ref), (kn_ref, vn_ref)):
        probs.append(jnp.exp(contract(k_ref[...], q, 1, 1) * SCALE - logsum))
        d_probs.append(contract(v_ref[...], grad, 1, 1))
    inner = sum(jnp.sum(p * d, axis=0, keepdims=True) for p, d in zip(probs, d_probs))
    dq = 0.0
    for at, k_ref in enumerate((kh_ref, kn_ref)):
        d_scores = (probs[at] * (d_probs[at] - inner)).astype(BF)
        dq = dq + contract(k_ref[...], d_scores, 0, 0)
        dk = contract(d_scores, q, 1, 0)
        dv = contract(probs[at].astype(BF), grad, 1, 0)

        @pl.when(step == 0)
        def _():
            sums[at][...] = dk
            sums[2 + at][...] = dv

        @pl.when(step > 0)
        def _():
            sums[at][...] += dk
            sums[2 + at][...] += dv
    dq_ref[...] = (dq * SCALE).T.astype(BF)

    @pl.when(step == pl.num_programs(1) - 1)
    def _():
        dkh_ref[...] = (sums[0][...] * SCALE).astype(BF)
        dkn_ref[...] = (sums[1][...] * SCALE).astype(BF)
        dvh_ref[...] = sums[2][...].astype(BF)
        dvn_ref[...] = sums[3][...].astype(BF)


def kv_specs(rows, heads):
    k = pl.BlockSpec((rows, DH), lambda h, b: (0, h))
    v = pl.BlockSpec((rows, DH), lambda h, b: (0, heads + h))
    return k, k, v, v


def attention(q, kvh, kvn, block=None):
    rows, width = q.shape
    block = block or rows
    heads = width // DH
    row = pl.BlockSpec((block, DH), lambda h, b: (b, h))
    log = pl.BlockSpec((1, 1, block), lambda h, b: (h, 0, b))
    return pl.pallas_call(forward_kernel, grid=(heads, rows // block),
        in_specs=[row, *kv_specs(kvh.shape[0], heads)], out_specs=[row, log],
        out_shape=[jax.ShapeDtypeStruct((rows, width), BF), jax.ShapeDtypeStruct((heads, 1, rows), F32)],
        name="attention_forward")(q, kvh, kvn, kvh, kvn)


def attention_back(q, kvh, kvn, grad, logsum, block=None):
    rows, width = q.shape
    block = block or rows
    heads = width // DH
    keys = kvh.shape[0]
    row = pl.BlockSpec((block, DH), lambda h, b: (b, h))
    log = pl.BlockSpec((1, 1, block), lambda h, b: (h, 0, b))
    k = pl.BlockSpec((keys, DH), lambda h, b: (0, h))
    return pl.pallas_call(backward_kernel, grid=(heads, rows // block),
        in_specs=[row, *kv_specs(keys, heads), row, log],
        out_specs=[row, k, k, k, k],
        out_shape=[jax.ShapeDtypeStruct((rows, width), BF)] + [jax.ShapeDtypeStruct((keys, width), BF)] * 4,
        scratch_shapes=[pltpu.VMEM((keys, DH), F32)] * 4,
        name="attention_backward")(q, kvh, kvn, kvh, kvn, grad, logsum)


def sum_kernel(*refs):
    count = (len(refs) - 1) // 2
    total = 0.0
    for at in range(count):
        total = total + contract(refs[at][...], refs[count + at][...], 1, 1)
    refs[-1][...] = total.astype(refs[-1].dtype)


def sum_products(lefts, rights, block=256):
    rows = lefts[0].shape[0]
    width = rights[0].shape[0]
    return pl.pallas_call(
        sum_kernel,
        grid=(width // block,),
        in_specs=[pl.BlockSpec(left.shape, lambda n: (0, 0)) for left in lefts]
        + [pl.BlockSpec((block, right.shape[1]), lambda n: (n, 0)) for right in rights],
        out_specs=pl.BlockSpec((rows, block), lambda n: (0, n)),
        out_shape=jax.ShapeDtypeStruct((rows, width), BF),
        name="sum_products",
    )(*lefts, *rights)


def after(value, *others):
    return lax.optimization_barrier((value,) + others)[0]


def across(array, step, axis="ctx"):
    size = lax.axis_size(axis)
    return lax.ppermute(array, axis, [(at, at ^ step) for at in range(size)])


def collect(piece):
    return lax.all_gather(piece, "shard", axis=0, tiled=True)


def scatter(total):
    mine = lax.psum_scatter(total, "shard", scatter_dimension=0, tiled=True)
    return with_layout_constraint(mine, Layout((0, 1)))


def scatter_direct(total):
    size = lax.axis_size("shard")
    rows = total.shape[0] // size
    index = lax.axis_index("shard")

    def block(step):
        return lax.dynamic_slice_in_dim(total, ((index + step) % size) * rows, rows, 0)

    got = [
        lax.ppermute(block(step), "shard", [(at, (at + step) % size) for at in range(size)])
        for step in range(1, size)
    ]
    return block(0), got


def sum_direct(mine, got):
    total = sum([item.astype(F32) for item in got], mine.astype(F32)).astype(BF)
    return with_layout_constraint(total, Layout((0, 1)))


def fill(own, far):
    return [own, across(own, 1), far, across(far, 1)]


def spread(own):
    return fill(own, across(own, 2))


def near_sums(parts):
    return [
        (parts[q].astype(F32) + across(parts[q + 1], 1).astype(F32)).astype(BF) for q in (0, 2)
    ]


def far_sum(own, far, *hold):
    got = across(far, 2)
    if hold:
        got = after(got, *hold)
    return (own.astype(F32) + got.astype(F32)).astype(BF)


def halves(array):
    width = array.shape[1] // 2
    return [array[:, :width], array[:, width:]]


def join_pair(own, far):
    return fill(far_sum(own, far), far_sum(far, own))


def ordered(pieces, bits):
    low, high = bits
    swapped = [jnp.where(high, pieces[q ^ 2], pieces[q]) for q in range(4)]
    return [jnp.where(low, swapped[q ^ 1], swapped[q]) for q in range(4)]


def tp_sum(low):
    return low.astype(F32) + across(low, 1, "tp").astype(F32)


def butterfly(flat, axes):
    for axis in axes:
        step = 1
        while step < lax.axis_size(axis):
            flat = flat + across(flat, step, axis)
            step *= 2
    return flat


def shards(
    inputs,
    cotangent,
    query_weight,
    key_weight,
    value_weight,
    output_weight,
    up_weight,
    down_weight,
    query_value_bias,
    up_bias,
    norm_gains,
    other_biases,
):
    local_rows = inputs.shape[1]
    member = lax.axis_index("ctx")
    relative = jnp.arange(4) ^ member
    bits = ((member & 1) == 1, (member & 2) == 2)
    n_shard = lax.axis_size("shard")
    n_tp = lax.axis_size("tp")

    def own_columns(weight, step=0):
        width = weight.shape[1] // 4
        return lax.dynamic_slice_in_dim(weight, (member ^ step) * width, width, 1)

    tokens = inputs.reshape(local_rows, D)
    tokens_far = across(tokens, 2)
    grad_out = cotangent.reshape(local_rows, D).astype(F32)

    small = (query_value_bias, norm_gains, other_biases, up_bias)
    packed = jnp.concatenate([item.reshape(1, -1) for item in small], axis=1)
    tp_index = lax.axis_index("tp")
    slot = lax.axis_index("shard") * n_tp + tp_index
    packed_all = lax.dynamic_update_slice_in_dim(
        jnp.zeros((n_shard * n_tp, packed.shape[1]), BF), packed, slot, 0
    )
    packed_all = butterfly(packed_all, ("tp", "shard"))
    packed_all = packed_all.reshape(n_shard, n_tp, packed.shape[1])
    at = 0
    small_all = []
    for item in small:
        part = packed_all[:, :, at : at + item.size].reshape((n_shard, n_tp) + item.shape)
        at += item.size
        small_all.append(part)
    qv_all = lax.dynamic_index_in_dim(small_all[0], tp_index, 1, False)
    qv_half = qv_all.transpose(1, 2, 0, 3).reshape(2, 4, -1).astype(F32)
    qv_vector = jnp.take(qv_half, relative, axis=1)
    gains = small_all[1].transpose(2, 1, 3, 0, 4).reshape(2, D).astype(F32)
    biases = small_all[2].transpose(2, 1, 3, 0, 4).reshape(4, D).astype(F32)
    up_all = lax.dynamic_index_in_dim(small_all[3], tp_index, 1, False)
    up_vector = jnp.take(up_all.transpose(1, 0, 2).reshape(4, -1).astype(F32), relative, axis=0)

    kv_width = key_weight.shape[1] // 4
    heads_each = kv_width // DH
    heads_here = 4 * heads_each
    ff_half = up_weight.shape[1] // 8
    kv_own = collect(jnp.concatenate([own_columns(key_weight), own_columns(value_weight)], axis=1))
    pair_own = collect(
        jnp.concatenate([own_columns(query_weight), own_columns(output_weight)], axis=1)
    )
    up_piece = own_columns(up_weight)
    down_piece = own_columns(down_weight)
    up_own = [collect(up_piece[:, half * ff_half : (half + 1) * ff_half]) for half in range(2)]
    down_own = [collect(down_piece[:, half * ff_half : (half + 1) * ff_half]) for half in range(2)]
    ff_part = ff_half // 2
    down_far = collect(own_columns(down_weight, 2)[:, ff_half + ff_part :])
    key_value_w = fill(kv_own, across(after(kv_own, tokens_far), 2))
    pair_far = after(across(pair_own, 2), kv_own)
    pair_w = fill(pair_own, pair_far)
    query_w = [item[:, :kv_width] for item in pair_w]
    output_w = [item[:, kv_width:] for item in pair_w]

    tokens_two = jnp.concatenate([tokens, tokens_far], axis=0)
    zero_row = jnp.zeros((kv_width,), F32)
    kv_here = [
        (
            product(tokens_two, key_value_w[q]) + jnp.concatenate([zero_row, qv_vector[1, q]])
        ).astype(BF)
        for q in range(4)
    ]
    kv_near = [across(kv_here[q ^ 1], 1) for q in range(4)]
    queries = [(product(tokens, query_w[q]) + qv_vector[0, q]).astype(BF) for q in range(4)]
    attended, logsums = [], []
    for q in range(4):
        out, log = attention(queries[q], kv_here[q], kv_near[q])
        attended.append(out)
        logsums.append(log)
    attn_low = sum_products(attended, output_w)
    up_far = across(up_own[0], 2)
    up_w = [fill(up_own[0], up_far), spread(after(up_own[1], attended[3]))]
    attn_branch = tp_sum(attn_low) + biases[0]
    normed_one, factor_one = normalize(tokens.astype(F32) + attn_branch)
    hidden_one = normed_one * gains[0] + biases[1]
    hidden_low = hidden_one.astype(BF)

    pairs = [(half, q) for half in range(2) for q in range(4)]
    up_rows = up_vector.reshape(4, 2, ff_half)
    pre_act = [product(hidden_low, up_w[half][q]) + up_rows[q, half] for half, q in pairs]
    activated = [gelu_tanh(item).astype(BF) for item in pre_act]
    down_swapped = across(after(down_own[1], activated[0])[:, :ff_part], 2)
    down_last = jnp.concatenate([down_swapped, after(down_far, *activated)], axis=1)
    down_w = [
        spread(after(down_own[0], attn_low)),
        fill(down_own[1], down_last),
    ]
    mlp_low = sum_products(activated, [down_w[half][q] for half, q in pairs])
    mlp_branch = tp_sum(mlp_low) + biases[2]
    second = hidden_one + mlp_branch
    normed_two, factor_two = normalize(second)
    result = normed_two * gains[1] + biases[3]
    grad_second = norm_backward(grad_out * gains[1], normed_two, factor_two)
    grad_mlp = grad_second.astype(BF)
    down_parts = [transposed_times(grad_mlp, item).astype(BF) for item in activated]
    down_late = near_sums(down_parts[4:8])
    down_early = near_sums(down_parts[0:4])
    down_late = jnp.concatenate(down_late, axis=1)
    grad_mlp_then = after(grad_mlp, down_late, *down_early)
    down_second = scatter(down_late)
    grad_pre = []
    for at, (half, q) in enumerate(pairs):
        _, gelu_pull = jax.vjp(gelu_tanh, pre_act[at])
        grad_pre.append(gelu_pull(product(grad_mlp_then, down_w[half][q]))[0].astype(BF))
    hidden_part = sum_products(grad_pre, [up_w[half][q] for half, q in pairs])
    down_total = far_sum(*down_early, hidden_part)
    down_first = scatter(down_total)
    up_parts = [transposed_times(hidden_low, item).astype(BF) for item in grad_pre]
    up_early = near_sums(up_parts[0:4])
    up_late = jnp.concatenate(near_sums(up_parts[4:8]), axis=1)
    up_second = scatter(up_late)
    hidden_got = after(across(hidden_part, 1, "tp"), down_total, up_late, *up_early)
    grad_hidden = grad_second + (hidden_part.astype(F32) + hidden_got.astype(F32))
    down_second = halves(down_second)
    down_pair = [far_sum(*down_second), far_sum(*down_second[::-1])]
    grad_first = norm_backward(grad_hidden * gains[0], normed_one, factor_one)
    grad_branch = grad_first.astype(BF)
    grad_attended = [product(grad_branch, output_w[q]).astype(BF) for q in range(4)]
    up_total = far_sum(*up_early, grad_branch)
    up_first = scatter(up_total)
    output_early = near_sums(
        [transposed_times(grad_branch, attended[q]).astype(BF) for q in range(4)]
    )
    grad_attended[1:] = lax.optimization_barrier((*grad_attended[1:], *output_early))[:3]
    grad_attended[2:] = lax.optimization_barrier((*grad_attended[2:], up_total))[:-1]
    down_far_first = across(down_first, 2)
    grad_q, here_parts, near_parts = [], [], []
    for q in range(4):
        dq, dk_here, dk_near, dv_here, dv_near = attention_back(
            queries[q], kv_here[q], kv_near[q], grad_attended[q], logsums[q]
        )
        grad_q.append(dq)
        here_parts.append((dk_here, dv_here))
        near_parts.append((across(dk_near, 1), across(dv_near, 1)))
    two_sums = [
        jnp.concatenate(
            [
                (here_parts[q][at].astype(F32) + near_parts[q ^ 1][at].astype(F32)).astype(BF)
                for at in range(2)
            ],
            axis=1,
        )
        for q in range(4)
    ]
    far_sums = [across(two_sums[q][local_rows:], 2) for q in range(4)]
    far_sums = lax.optimization_barrier((*far_sums, *two_sums))[:4]
    grad_kv = [
        (two_sums[q][:local_rows].astype(F32) + far_sums[q ^ 2].astype(F32)).astype(BF)
        for q in range(4)
    ]
    output_direct = scatter_direct(far_sum(*output_early, *grad_q))
    query_early = near_sums([transposed_times(tokens, grad_q[q]).astype(BF) for q in range(4)])
    kv_parts = [transposed_times(tokens, grad_kv[q]).astype(BF) for q in range(4)]
    kv_early = near_sums(kv_parts)
    kv_got = across(kv_early[1], 2)
    kv_total = (kv_early[0].astype(F32) + kv_got.astype(F32)).astype(BF)
    kv_mine = scatter(kv_total)
    query_far = after(across(after(query_early[1], *grad_kv), 2), *kv_early)
    query_total = (query_early[0].astype(F32) + query_far.astype(F32)).astype(BF)
    query_mine, query_got = scatter_direct(query_total)
    output_mine, output_got = lax.optimization_barrier((*output_direct, kv_total))[:2]
    up_first, up_second, grad_q_then = (
        after(item, kv_total) for item in (up_first, up_second, grad_q[0])
    )
    down_grads = [fill(down_first, down_far_first), fill(*down_pair)]
    up_grads = [spread(up_first), join_pair(*halves(up_second))]
    output_grads = spread(sum_direct(output_mine, output_got))
    query_grads = spread(sum_direct(query_mine, query_got))
    kv_grads = spread(kv_mine)
    input_part = sum_products([grad_q_then] + grad_q[1:] + grad_kv, query_w + key_value_w)
    input_grad = grad_first + tp_sum(input_part)

    def canonical(rows):
        return jnp.take(jnp.stack(rows), relative, axis=0).reshape(-1)

    def column_sums(array):
        return jnp.sum(array.astype(F32), axis=0)

    pieces = [
        canonical([column_sums(grad_q[q]) for q in range(4)]),
        canonical([column_sums(grad_kv[q][:, kv_width:]) for q in range(4)]),
        canonical(
            [
                jnp.concatenate([column_sums(grad_pre[q]), column_sums(grad_pre[4 + q])])
                for q in range(4)
            ]
        ),
        jnp.sum(grad_hidden * normed_one, axis=0),
        jnp.sum(grad_out * normed_two, axis=0),
        column_sums(grad_branch),
        jnp.sum(grad_hidden, axis=0),
        column_sums(grad_mlp),
        jnp.sum(grad_out, axis=0),
        jnp.stack(
            [
                jnp.sum(second * second),
                jnp.sum(attn_branch * attn_branch),
                jnp.sum(mlp_branch * mlp_branch),
            ]
        ),
    ]
    sizes = [item.shape[0] for item in pieces]
    flat = jnp.concatenate(pieces + [jnp.zeros((-sum(sizes) % 1024,), F32)]).reshape(-1, 128)
    flat = butterfly(after(flat, *kv_early), ("ctx", "shard")).reshape(-1)
    totals = []
    at = 0
    for size in sizes:
        totals.append(flat[at : at + size])
        at += size
    shard_index = lax.axis_index("shard")
    piece = DH // n_shard
    heads_part = H // n_tp

    def last_piece(array, axis):
        return lax.dynamic_slice_in_dim(array, shard_index * piece, piece, axis)

    grad_qv_bias = last_piece(jnp.stack(totals[0:2]).reshape(2, heads_here, DH), 2)
    grad_up_bias = last_piece(totals[2].reshape(-1, DH), 1)

    def feature_rows(rows):
        stacked = jnp.stack(rows).reshape(len(rows), H, DH)
        return last_piece(
            lax.dynamic_slice_in_dim(stacked, tp_index * heads_part, heads_part, 1), 2
        )

    grad_gains = feature_rows(totals[3:5])
    grad_biases = feature_rows(totals[5:9])
    count_all = local_rows * n_shard * lax.axis_size("ctx") * D
    root_squares = jnp.sqrt(totals[9] / count_all)

    def whole(parts):
        return jnp.concatenate(ordered(parts, bits), axis=1).astype(F32)

    def whole_halves(parts):
        placed = [ordered(half, bits) for half in parts]
        return jnp.concatenate(
            [placed[half][q] for q in range(4) for half in range(2)], axis=1
        ).astype(F32)

    return (
        result.astype(BF).reshape(1, local_rows, D),
        input_grad.astype(BF).reshape(1, local_rows, D),
        whole(query_grads),
        whole([item[:, :kv_width] for item in kv_grads]),
        whole([item[:, kv_width:] for item in kv_grads]),
        whole(output_grads),
        whole_halves(up_grads),
        whole_halves(down_grads),
        grad_qv_bias,
        grad_up_bias,
        grad_gains,
        grad_biases,
        root_squares,
    )


def solution(mesh):
    if mesh.shape["ctx"] != 4 or mesh.shape["tp"] != 2:
        raise ValueError("unexpected mesh")
    placed = (
        P("shard", "ctx", None),
        P("shard", "ctx", None),
        P("shard", "tp"),
        P("shard", "tp"),
        P("shard", "tp"),
        P("shard", "tp"),
        P("shard", "tp"),
        P("shard", "tp"),
        P(None, "tp", "shard"),
        P("tp", "shard"),
        P(None, "tp", "shard"),
        P(None, "tp", "shard"),
    )
    return jax.shard_map(
        shards,
        mesh=mesh,
        in_specs=placed,
        out_specs=(
            P("shard", "ctx", None),
            P("shard", "ctx", None),
            P("shard", "tp"),
            P("shard", "tp"),
            P("shard", "tp"),
            P("shard", "tp"),
            P("shard", "tp"),
            P("shard", "tp"),
            P(None, "tp", "shard"),
            P("tp", "shard"),
            P(None, "tp", "shard"),
            P(None, "tp", "shard"),
            P(),
        ),
        check_vma=False,
    )
```

```python
import jax
import jax.numpy as jnp
from jax import lax
from jax.experimental import pallas as pl
from jax.experimental.pallas import tpu as pltpu
from jax.experimental.layout import Layout, with_layout_constraint
from jax.sharding import PartitionSpec as P


D = 2048
H = 16
DH = 128
SCALE = DH ** (-0.5)
BF = jnp.bfloat16
F32 = jnp.float32


epsilon = 1e-12


def product(left, right):
    return jnp.dot(left, right, preferred_element_type=F32)


def transposed_times(left, right):
    return lax.dot_general(left, right, (((0,), (0,)), ((), ())), preferred_element_type=F32)


def normalize(stream):
    center = stream - jnp.mean(stream, axis=-1, keepdims=True)
    factor = lax.rsqrt(jnp.mean(center * center, axis=-1, keepdims=True) + epsilon)
    return (center * factor, factor)


def norm_backward(grad_norm, normed, factor):
    return factor * (
        grad_norm
        - jnp.mean(grad_norm, axis=-1, keepdims=True)
        - normed * jnp.mean(grad_norm * normed, axis=-1, keepdims=True)
    )


def gelu_tanh(values):
    return jax.nn.gelu(values, approximate=True)


def contract(left, right, left_axis, right_axis):
    return lax.dot_general(
        left, right, (((left_axis,), (right_axis,)), ((), ())), preferred_element_type=F32
    )


def forward_kernel(q_ref, kh_ref, kn_ref, vh_ref, vn_ref, out_ref, log_ref):
    q = q_ref[...]
    near = contract(kh_ref[...], q, 1, 1) * SCALE
    far = contract(kn_ref[...], q, 1, 1) * SCALE
    peak = jnp.maximum(jnp.max(near, axis=0, keepdims=True), jnp.max(far, axis=0, keepdims=True))
    near = jnp.exp(near - peak)
    far = jnp.exp(far - peak)
    total = jnp.sum(near, axis=0, keepdims=True) + jnp.sum(far, axis=0, keepdims=True)
    out = contract(vh_ref[...], near.astype(BF), 0, 0) + contract(vn_ref[...], far.astype(BF), 0, 0)
    out_ref[...] = (out / total).T.astype(BF)
    log_ref[0] = peak + jnp.log(total)


def backward_kernel(q_ref, kh_ref, kn_ref, vh_ref, vn_ref, grad_ref, log_ref, dq_ref, dkh_ref, dkn_ref, dvh_ref, dvn_ref, *sums):
    step = pl.program_id(1)
    q = q_ref[...]
    grad = grad_ref[...]
    logsum = log_ref[0]
    probs, d_probs = [], []
    for k_ref, v_ref in ((kh_ref, vh_ref), (kn_ref, vn_ref)):
        probs.append(jnp.exp(contract(k_ref[...], q, 1, 1) * SCALE - logsum))
        d_probs.append(contract(v_ref[...], grad, 1, 1))
    inner = sum(jnp.sum(p * d, axis=0, keepdims=True) for p, d in zip(probs, d_probs))
    dq = 0.0
    for at, k_ref in enumerate((kh_ref, kn_ref)):
        d_scores = (probs[at] * (d_probs[at] - inner)).astype(BF)
        dq = dq + contract(k_ref[...], d_scores, 0, 0)
        dk = contract(d_scores, q, 1, 0)
        dv = contract(probs[at].astype(BF), grad, 1, 0)

        @pl.when(step == 0)
        def _():
            sums[at][...] = dk
            sums[2 + at][...] = dv

        @pl.when(step > 0)
        def _():
            sums[at][...] += dk
            sums[2 + at][...] += dv
    dq_ref[...] = (dq * SCALE).T.astype(BF)

    @pl.when(step == pl.num_programs(1) - 1)
    def _():
        dkh_ref[...] = (sums[0][...] * SCALE).astype(BF)
        dkn_ref[...] = (sums[1][...] * SCALE).astype(BF)
        dvh_ref[...] = sums[2][...].astype(BF)
        dvn_ref[...] = sums[3][...].astype(BF)


def kv_specs(rows, heads):
    k = pl.BlockSpec((rows, DH), lambda h, b: (0, h))
    v = pl.BlockSpec((rows, DH), lambda h, b: (0, heads + h))
    return k, k, v, v


def attention(q, kvh, kvn, block=None):
    rows, width = q.shape
    block = block or rows
    heads = width // DH
    row = pl.BlockSpec((block, DH), lambda h, b: (b, h))
    log = pl.BlockSpec((1, 1, block), lambda h, b: (h, 0, b))
    return pl.pallas_call(forward_kernel, grid=(heads, rows // block),
        in_specs=[row, *kv_specs(kvh.shape[0], heads)], out_specs=[row, log],
        out_shape=[jax.ShapeDtypeStruct((rows, width), BF), jax.ShapeDtypeStruct((heads, 1, rows), F32)],
        name="attention_forward")(q, kvh, kvn, kvh, kvn)


def attention_back(q, kvh, kvn, grad, logsum, block=None):
    rows, width = q.shape
    block = block or rows
    heads = width // DH
    keys = kvh.shape[0]
    row = pl.BlockSpec((block, DH), lambda h, b: (b, h))
    log = pl.BlockSpec((1, 1, block), lambda h, b: (h, 0, b))
    k = pl.BlockSpec((keys, DH), lambda h, b: (0, h))
    return pl.pallas_call(backward_kernel, grid=(heads, rows // block),
        in_specs=[row, *kv_specs(keys, heads), row, log],
        out_specs=[row, k, k, k, k],
        out_shape=[jax.ShapeDtypeStruct((rows, width), BF)] + [jax.ShapeDtypeStruct((keys, width), BF)] * 4,
        scratch_shapes=[pltpu.VMEM((keys, DH), F32)] * 4,
        name="attention_backward")(q, kvh, kvn, kvh, kvn, grad, logsum)


def sum_kernel(*refs):
    count = (len(refs) - 1) // 2
    total = 0.0
    for at in range(count):
        total = total + contract(refs[at][...], refs[count + at][...], 1, 1)
    refs[-1][...] = total.astype(refs[-1].dtype)


def sum_products(lefts, rights, block=256):
    rows = lefts[0].shape[0]
    width = rights[0].shape[0]
    return pl.pallas_call(
        sum_kernel,
        grid=(width // block,),
        in_specs=[pl.BlockSpec(left.shape, lambda n: (0, 0)) for left in lefts]
        + [pl.BlockSpec((block, right.shape[1]), lambda n: (n, 0)) for right in rights],
        out_specs=pl.BlockSpec((rows, block), lambda n: (0, n)),
        out_shape=jax.ShapeDtypeStruct((rows, width), BF),
        name="sum_products",
    )(*lefts, *rights)


def after(value, *others):
    return lax.optimization_barrier((value,) + others)[0]


def across(array, step, axis="ctx"):
    size = lax.axis_size(axis)
    return lax.ppermute(array, axis, [(at, at ^ step) for at in range(size)])


def collect(piece):
    return lax.all_gather(piece, "shard", axis=0, tiled=True)


def scatter(total):
    mine = lax.psum_scatter(total, "shard", scatter_dimension=0, tiled=True)
    return with_layout_constraint(mine, Layout((0, 1)))


def scatter_direct(total):
    size = lax.axis_size("shard")
    rows = total.shape[0] // size
    index = lax.axis_index("shard")

    def block(step):
        return lax.dynamic_slice_in_dim(total, ((index + step) % size) * rows, rows, 0)

    got = [
        lax.ppermute(block(step), "shard", [(at, (at + step) % size) for at in range(size)])
        for step in range(1, size)
    ]
    return block(0), got


def sum_direct(mine, got):
    total = sum([item.astype(F32) for item in got], mine.astype(F32)).astype(BF)
    return with_layout_constraint(total, Layout((0, 1)))


def fill(own, far):
    return [own, across(own, 1), far, across(far, 1)]


def spread(own):
    return fill(own, across(own, 2))


def near_sums(parts):
    return [
        (parts[q].astype(F32) + across(parts[q + 1], 1).astype(F32)).astype(BF) for q in (0, 2)
    ]


def far_sum(own, far, *hold):
    got = across(far, 2)
    if hold:
        got = after(got, *hold)
    return (own.astype(F32) + got.astype(F32)).astype(BF)


def halves(array):
    width = array.shape[1] // 2
    return [array[:, :width], array[:, width:]]


def join_pair(own, far):
    return fill(far_sum(own, far), far_sum(far, own))


def ordered(pieces, bits):
    low, high = bits
    swapped = [jnp.where(high, pieces[q ^ 2], pieces[q]) for q in range(4)]
    return [jnp.where(low, swapped[q ^ 1], swapped[q]) for q in range(4)]


def tp_sum(low):
    return low.astype(F32) + across(low, 1, "tp").astype(F32)


def butterfly(flat, axes):
    for axis in axes:
        step = 1
        while step < lax.axis_size(axis):
            flat = flat + across(flat, step, axis)
            step *= 2
    return flat


def shards(
    inputs,
    cotangent,
    query_weight,
    key_weight,
    value_weight,
    output_weight,
    up_weight,
    down_weight,
    query_value_bias,
    up_bias,
    norm_gains,
    other_biases,
):
    local_rows = inputs.shape[1]
    member = lax.axis_index("ctx")
    relative = jnp.arange(4) ^ member
    bits = ((member & 1) == 1, (member & 2) == 2)
    n_shard = lax.axis_size("shard")
    n_tp = lax.axis_size("tp")

    def own_columns(weight, step=0):
        width = weight.shape[1] // 4
        return lax.dynamic_slice_in_dim(weight, (member ^ step) * width, width, 1)

    tokens = inputs.reshape(local_rows, D)
    tokens_far = across(tokens, 2)
    grad_out = cotangent.reshape(local_rows, D).astype(F32)

    small = (query_value_bias, norm_gains, other_biases, up_bias)
    packed = jnp.concatenate([item.reshape(1, -1) for item in small], axis=1)
    tp_index = lax.axis_index("tp")
    slot = lax.axis_index("shard") * n_tp + tp_index
    packed_all = lax.dynamic_update_slice_in_dim(
        jnp.zeros((n_shard * n_tp, packed.shape[1]), BF), packed, slot, 0
    )
    packed_all = butterfly(packed_all, ("tp", "shard"))
    packed_all = packed_all.reshape(n_shard, n_tp, packed.shape[1])
    at = 0
    small_all = []
    for item in small:
        part = packed_all[:, :, at : at + item.size].reshape((n_shard, n_tp) + item.shape)
        at += item.size
        small_all.append(part)
    qv_all = lax.dynamic_index_in_dim(small_all[0], tp_index, 1, False)
    qv_half = qv_all.transpose(1, 2, 0, 3).reshape(2, 4, -1).astype(F32)
    qv_vector = jnp.take(qv_half, relative, axis=1)
    gains = small_all[1].transpose(2, 1, 3, 0, 4).reshape(2, D).astype(F32)
    biases = small_all[2].transpose(2, 1, 3, 0, 4).reshape(4, D).astype(F32)
    up_all = lax.dynamic_index_in_dim(small_all[3], tp_index, 1, False)
    up_vector = jnp.take(up_all.transpose(1, 0, 2).reshape(4, -1).astype(F32), relative, axis=0)

    kv_width = key_weight.shape[1] // 4
    heads_each = kv_width // DH
    heads_here = 4 * heads_each
    ff_half = up_weight.shape[1] // 8
    kv_own = collect(jnp.concatenate([own_columns(key_weight), own_columns(value_weight)], axis=1))
    pair_own = collect(
        jnp.concatenate([own_columns(query_weight), own_columns(output_weight)], axis=1)
    )
    up_piece = own_columns(up_weight)
    down_piece = own_columns(down_weight)
    up_own = [collect(up_piece[:, half * ff_half : (half + 1) * ff_half]) for half in range(2)]
    down_own = [collect(down_piece[:, half * ff_half : (half + 1) * ff_half]) for half in range(2)]
    ff_part = ff_half // 2
    down_far = collect(own_columns(down_weight, 2)[:, ff_half + ff_part :])
    key_value_w = fill(kv_own, across(after(kv_own, tokens_far), 2))
    pair_far = after(across(pair_own, 2), kv_own)
    pair_w = fill(pair_own, pair_far)
    query_w = [item[:, :kv_width] for item in pair_w]
    output_w = [item[:, kv_width:] for item in pair_w]

    tokens_two = jnp.concatenate([tokens, tokens_far], axis=0)
    zero_row = jnp.zeros((kv_width,), F32)
    kv_here = [
        (
            product(tokens_two, key_value_w[q]) + jnp.concatenate([zero_row, qv_vector[1, q]])
        ).astype(BF)
        for q in range(4)
    ]
    kv_near = [across(kv_here[q ^ 1], 1) for q in range(4)]
    queries = [(product(tokens, query_w[q]) + qv_vector[0, q]).astype(BF) for q in range(4)]
    attended, logsums = [], []
    for q in range(4):
        out, log = attention(queries[q], kv_here[q], kv_near[q])
        attended.append(out)
        logsums.append(log)
    attn_low = sum_products(attended, output_w)
    up_far = across(up_own[0], 2)
    up_w = [fill(up_own[0], up_far), spread(after(up_own[1], attended[3]))]
    attn_branch = tp_sum(attn_low) + biases[0]
    normed_one, factor_one = normalize(tokens.astype(F32) + attn_branch)
    hidden_one = normed_one * gains[0] + biases[1]
    hidden_low = hidden_one.astype(BF)

    pairs = [(half, q) for half in range(2) for q in range(4)]
    up_rows = up_vector.reshape(4, 2, ff_half)
    pre_act = [product(hidden_low, up_w[half][q]) + up_rows[q, half] for half, q in pairs]
    activated = [gelu_tanh(item).astype(BF) for item in pre_act]
    down_held = after(down_own[1], activated[0])
    down_swapped = across(down_held[:, :ff_part], 2)
    down_last = jnp.concatenate([down_swapped, after(down_far, *activated)], axis=1)
    down_w = [
        spread(after(down_own[0], attn_low)),
        fill(down_held, down_last),
    ]
    mlp_low = sum_products(activated, [down_w[half][q] for half, q in pairs])
    mlp_branch = tp_sum(mlp_low) + biases[2]
    second = hidden_one + mlp_branch
    normed_two, factor_two = normalize(second)
    result = normed_two * gains[1] + biases[3]
    grad_second = norm_backward(grad_out * gains[1], normed_two, factor_two)
    grad_mlp = grad_second.astype(BF)
    down_parts = [transposed_times(grad_mlp, item).astype(BF) for item in activated]
    down_late = near_sums(down_parts[4:8])
    down_early = near_sums(down_parts[0:4])
    down_late = jnp.concatenate(down_late, axis=1)
    grad_mlp_then = after(grad_mlp, down_late, *down_early)
    down_second = scatter(down_late)
    grad_pre = []
    for at, (half, q) in enumerate(pairs):
        _, gelu_pull = jax.vjp(gelu_tanh, pre_act[at])
        grad_pre.append(gelu_pull(product(grad_mlp_then, down_w[half][q]))[0].astype(BF))
    hidden_part = sum_products(grad_pre, [up_w[half][q] for half, q in pairs])
    down_total = far_sum(*down_early, hidden_part)
    down_first = scatter(down_total)
    up_parts = [transposed_times(hidden_low, item).astype(BF) for item in grad_pre]
    up_early = near_sums(up_parts[0:4])
    up_late = jnp.concatenate(near_sums(up_parts[4:8]), axis=1)
    up_second = scatter(up_late)
    hidden_got = after(across(hidden_part, 1, "tp"), down_total, up_late, *up_early)
    grad_hidden = grad_second + (hidden_part.astype(F32) + hidden_got.astype(F32))
    down_second = halves(down_second)
    down_pair = [far_sum(*down_second), far_sum(*down_second[::-1])]
    grad_first = norm_backward(grad_hidden * gains[0], normed_one, factor_one)
    grad_branch = grad_first.astype(BF)
    grad_attended = [product(grad_branch, output_w[q]).astype(BF) for q in range(4)]
    up_total = far_sum(*up_early, grad_branch)
    up_first = scatter(up_total)
    output_early = near_sums(
        [transposed_times(grad_branch, attended[q]).astype(BF) for q in range(4)]
    )
    grad_attended[1:] = lax.optimization_barrier((*grad_attended[1:], *output_early))[:3]
    grad_attended[2:] = lax.optimization_barrier((*grad_attended[2:], up_total))[:-1]
    down_far_first = across(down_first, 2)
    grad_q, here_parts, near_parts = [], [], []
    for q in range(4):
        dq, dk_here, dk_near, dv_here, dv_near = attention_back(
            queries[q], kv_here[q], kv_near[q], grad_attended[q], logsums[q]
        )
        grad_q.append(dq)
        here_parts.append((dk_here, dv_here))
        near_parts.append((across(dk_near, 1), across(dv_near, 1)))
    two_sums = [
        jnp.concatenate(
            [
                (here_parts[q][at].astype(F32) + near_parts[q ^ 1][at].astype(F32)).astype(BF)
                for at in range(2)
            ],
            axis=1,
        )
        for q in range(4)
    ]
    far_sums = [across(two_sums[q][local_rows:], 2) for q in range(4)]
    far_sums = lax.optimization_barrier((*far_sums, *two_sums))[:4]
    grad_kv = [
        (two_sums[q][:local_rows].astype(F32) + far_sums[q ^ 2].astype(F32)).astype(BF)
        for q in range(4)
    ]
    output_direct = scatter_direct(far_sum(*output_early, *grad_q))
    query_early = near_sums([transposed_times(tokens, grad_q[q]).astype(BF) for q in range(4)])
    kv_parts = [transposed_times(tokens, grad_kv[q]).astype(BF) for q in range(4)]
    kv_early = near_sums(kv_parts)
    kv_got = across(kv_early[1], 2)
    kv_total = (kv_early[0].astype(F32) + kv_got.astype(F32)).astype(BF)
    kv_mine = scatter(kv_total)
    query_far = across(after(query_early[1], kv_total), 2)
    query_total = (query_early[0].astype(F32) + query_far.astype(F32)).astype(BF)
    query_mine, query_got = scatter_direct(query_total)
    output_mine, output_got = lax.optimization_barrier((*output_direct, kv_total))[:2]
    up_first, up_second, grad_q_then = (
        after(item, kv_total) for item in (up_first, up_second, grad_q[0])
    )
    down_grads = [fill(down_first, down_far_first), fill(*down_pair)]
    up_grads = [spread(up_first), join_pair(*halves(up_second))]
    output_grads = spread(sum_direct(output_mine, output_got))
    query_grads = spread(sum_direct(query_mine, query_got))
    kv_grads = spread(kv_mine)
    input_part = sum_products([grad_q_then] + grad_q[1:] + grad_kv, query_w + key_value_w)
    input_grad = grad_first + tp_sum(input_part)

    def canonical(rows):
        return jnp.take(jnp.stack(rows), relative, axis=0).reshape(-1)

    def column_sums(array):
        return jnp.sum(array.astype(F32), axis=0)

    pieces = [
        canonical([column_sums(grad_q[q]) for q in range(4)]),
        canonical([column_sums(grad_kv[q][:, kv_width:]) for q in range(4)]),
        canonical(
            [
                jnp.concatenate([column_sums(grad_pre[q]), column_sums(grad_pre[4 + q])])
                for q in range(4)
            ]
        ),
        jnp.sum(grad_hidden * normed_one, axis=0),
        jnp.sum(grad_out * normed_two, axis=0),
        column_sums(grad_branch),
        jnp.sum(grad_hidden, axis=0),
        column_sums(grad_mlp),
        jnp.sum(grad_out, axis=0),
        jnp.stack(
            [
                jnp.sum(second * second),
                jnp.sum(attn_branch * attn_branch),
                jnp.sum(mlp_branch * mlp_branch),
            ]
        ),
    ]
    sizes = [item.shape[0] for item in pieces]
    flat = jnp.concatenate(pieces + [jnp.zeros((-sum(sizes) % 1024,), F32)]).reshape(-1, 128)
    flat = butterfly(after(flat, *kv_early), ("ctx", "shard")).reshape(-1)
    totals = []
    at = 0
    for size in sizes:
        totals.append(flat[at : at + size])
        at += size
    shard_index = lax.axis_index("shard")
    piece = DH // n_shard
    heads_part = H // n_tp

    def last_piece(array, axis):
        return lax.dynamic_slice_in_dim(array, shard_index * piece, piece, axis)

    grad_qv_bias = last_piece(jnp.stack(totals[0:2]).reshape(2, heads_here, DH), 2)
    grad_up_bias = last_piece(totals[2].reshape(-1, DH), 1)

    def feature_rows(rows):
        stacked = jnp.stack(rows).reshape(len(rows), H, DH)
        return last_piece(
            lax.dynamic_slice_in_dim(stacked, tp_index * heads_part, heads_part, 1), 2
        )

    grad_gains = feature_rows(totals[3:5])
    grad_biases = feature_rows(totals[5:9])
    count_all = local_rows * n_shard * lax.axis_size("ctx") * D
    root_squares = jnp.sqrt(totals[9] / count_all)

    def whole(parts):
        return jnp.concatenate(ordered(parts, bits), axis=1).astype(F32)

    def whole_halves(parts):
        placed = [ordered(half, bits) for half in parts]
        return jnp.concatenate(
            [placed[half][q] for q in range(4) for half in range(2)], axis=1
        ).astype(F32)

    return (
        result.astype(BF).reshape(1, local_rows, D),
        input_grad.astype(BF).reshape(1, local_rows, D),
        whole(query_grads),
        whole([item[:, :kv_width] for item in kv_grads]),
        whole([item[:, kv_width:] for item in kv_grads]),
        whole(output_grads),
        whole_halves(up_grads),
        whole_halves(down_grads),
        grad_qv_bias,
        grad_up_bias,
        grad_gains,
        grad_biases,
        root_squares,
    )


def solution(mesh):
    if mesh.shape["ctx"] != 4 or mesh.shape["tp"] != 2:
        raise ValueError("unexpected mesh")
    placed = (
        P("shard", "ctx", None),
        P("shard", "ctx", None),
        P("shard", "tp"),
        P("shard", "tp"),
        P("shard", "tp"),
        P("shard", "tp"),
        P("shard", "tp"),
        P("shard", "tp"),
        P(None, "tp", "shard"),
        P("tp", "shard"),
        P(None, "tp", "shard"),
        P(None, "tp", "shard"),
    )
    return jax.shard_map(
        shards,
        mesh=mesh,
        in_specs=placed,
        out_specs=(
            P("shard", "ctx", None),
            P("shard", "ctx", None),
            P("shard", "tp"),
            P("shard", "tp"),
            P("shard", "tp"),
            P("shard", "tp"),
            P("shard", "tp"),
            P("shard", "tp"),
            P(None, "tp", "shard"),
            P("tp", "shard"),
            P(None, "tp", "shard"),
            P(None, "tp", "shard"),
            P(),
        ),
        check_vma=False,
    )
```
